32 devices in a mesh: shot: 8 (over z, y), xy: 4 (over x, core).
Axes of the slice: x: 2, y: 2, z: 4, core: 2. Of those that a mesh axis runs over, the one named last changes fastest.
Arguments:
- fwd_prev: float32 [8, 32, 512, 128], P('shot', 'xy'), may hold values from -6 to 6
- fwd_cur: float32 [8, 32, 512, 128], P('shot', 'xy'), may hold values from -6 to 6
- bwd_next: float32 [8, 32, 512, 128], P('shot', 'xy'), may hold values from -6 to 6
- bwd_cur: float32 [8, 32, 512, 128], P('shot', 'xy'), may hold values from -6 to 6
- receiver_data: float32 [8, 7, 32, 512], P('shot', None, 'xy'), may hold values from -12 to 12
- velocity_term: float32 [32, 512, 128], P('xy'), may hold values from 0.05 to 0.25
- anisotropy: float32 [32, 512, 128], P('xy'), may hold values from 0 to 0.3
- wavelet: float32 [8, 7], replicated, may hold values from -16 to 16
- shot_x: int32 [8], replicated, may hold values from 0 to 31
- shot_y: int32 [8], replicated, may hold values from 0 to 511
- aperture: int32 [8, 2], replicated, may hold values from 0 to 3, all different within a row
- snap_steps: int32 [4], replicated, may hold values from 1 to 8, as said below
Outputs:
- image: float32 [32, 512, 128], P('xy', 'shot')
The draws below stay inside these ranges and needn't reach their ends.
Inputs may be any that keep to these rules, and one draw needn't show every extreme that they name: `snap_steps`: 4 distinct increasing times; the last is 8. `aperture`: each row names 2 distinct tiles.
All inputs are finite; a program needn't handle non-finite values.
Results may differ from the reference program's by a relative error of at most 0.0021.
Values may be sent and summed in bfloat16 or wider, within the bound.
No kernel may reach another device: no remote copies, remote signals or barrier semaphores. Data moves between devices by JAX's collectives and lax.ppermute only.
A program may use at most 128 MiB of HBM per device.

```python
import math
import jax
import jax.numpy as jnp
from jax import lax

CX = 8
NY = 512
NZ = 128
STEPS = 8
NSNAP = 4
SHOTS = 8
NX = 32
APER = 2
N_XY = 4


def draw_snap_steps(key, part):
    chosen = jax.random.permutation(key, STEPS - 1)[:NSNAP - 1] + 1
    joined = jnp.concatenate([chosen.astype(jnp.int32), jnp.full((1,), STEPS, jnp.int32)])
    return jnp.sort(joined).astype(jnp.int32)


def place_ends(result, stream_key, least, top_value):
    shape = result.shape
    place = [jax.random.randint(jax.random.fold_in(stream_key, axis), (), 0, shape[axis]) for axis in range(len(shape))]
    result = result.at[tuple(place)].set(least)
    longest = shape.index(max(shape))
    place[longest] = (place[longest] + 1) % shape[longest]
    return result.at[tuple(place)].set(top_value)


def shard_levels(key, extent, pieces, low, top_value):
    def one(axis_at, blocks):
        draws = jax.random.uniform(jax.random.fold_in(jax.random.fold_in(key, 6), axis_at), (blocks,), jnp.float32, low / len(pieces), top_value / len(pieces))
        return jnp.repeat(jnp.exp(draws), extent[axis_at] // blocks).reshape((-1,) + (1,) * (len(extent) - axis_at - 1))

    gain = one(*pieces[0])
    for cut in pieces[1:]:
        gain = gain * one(*cut)
    return gain


def different_ones(key, rows, count, top, lift):
    ranking = jax.random.permutation(jax.random.fold_in(key, 1), count)
    boost = ranking
    for power in range(3):
        boost = boost * boost // count
    boost = boost * lift // count
    tickets = jax.random.randint(jax.random.fold_in(key, 2), (rows, count), 0, 4096) + boost
    holders = jax.random.permutation(jax.random.fold_in(key, 3), rows)[jnp.arange(count) % rows]
    tickets = jnp.where(jnp.arange(rows)[:, None] == holders[None, :], 1 << 14, tickets)
    score = tickets * count + jnp.arange(count)
    return lax.top_k(score.astype(jnp.int32), top)[1].astype(jnp.int32)


def gaussian(rng, shape, scale, reach, split=(), kind=jnp.bfloat16):
    drawn = jax.random.normal(rng, shape, jnp.float32) * scale
    if len(split) > 0:
        drawn = shard_levels(rng, shape, split, -0.22, 0.18) * drawn
    return jnp.clip(drawn, min=-reach, max=reach).astype(kind)


def setup_inputs(seed: int = 0) -> dict:
    keys = jax.random.split(jax.random.key(seed), 13)
    fwd_prev = gaussian(keys[0], (SHOTS, NX, NY, NZ), 1.0, 6.0, ((0, 8), (1, 4)), jnp.float32)
    fwd_cur = gaussian(keys[1], (SHOTS, NX, NY, NZ), 1.0, 6.0, ((0, 8), (1, 4)), jnp.float32)
    bwd_next = gaussian(keys[2], (SHOTS, NX, NY, NZ), 1.0, 6.0, ((0, 8), (1, 4)), jnp.float32)
    bwd_cur = gaussian(keys[3], (SHOTS, NX, NY, NZ), 1.0, 6.0, ((0, 8), (1, 4)), jnp.float32)
    receiver_data = gaussian(keys[4], (SHOTS, STEPS - 1, NX, NY), 2.0, 12.0, ((0, 8), (2, 4)), jnp.float32)
    velocity_term = jnp.clip(jnp.exp(math.log(0.25) - 1.609438 * jax.random.uniform(keys[5], (NX, NY, NZ), jnp.float32) ** shard_levels(keys[5], (NX, NY, NZ), ((0, 4),), -0.2, 0.2)), 0.05, 0.25)
    anisotropy = jnp.clip(0.3 * jax.random.uniform(keys[6], (NX, NY, NZ), jnp.float32) ** shard_levels(keys[6], (NX, NY, NZ), ((0, 4),), -0.2, 0.2), 0.0, 0.3)
    wavelet = gaussian(keys[7], (SHOTS, STEPS - 1), 4.0, 16.0, (), jnp.float32)
    shot_x = place_ends(jax.random.randint(keys[8], (SHOTS,), 0, NX), jax.random.fold_in(keys[8], 1), 0, NX - 1).astype(jnp.int32)
    shot_y = place_ends(jax.random.randint(keys[9], (SHOTS,), 0, NY), jax.random.fold_in(keys[9], 1), 0, NY - 1).astype(jnp.int32)
    aperture = different_ones(keys[10], SHOTS, N_XY, APER, 8192)
    snap_steps = draw_snap_steps(jax.random.fold_in(keys[12], 71), 0)
    return {"fwd_prev": fwd_prev, "fwd_cur": fwd_cur, "bwd_next": bwd_next, "bwd_cur": bwd_cur, "receiver_data": receiver_data, "velocity_term": velocity_term, "anisotropy": anisotropy, "wavelet": wavelet, "shot_x": shot_x, "shot_y": shot_y, "aperture": aperture, "snap_steps": snap_steps}


def laplace(field, horizontal):
    padded = jnp.pad(field, 1)
    lateral = padded[2:, 1:-1, 1:-1] + padded[:-2, 1:-1, 1:-1] + padded[1:-1, 2:, 1:-1] + padded[1:-1, :-2, 1:-1] - 4.0 * field
    vertical = padded[1:-1, 1:-1, 2:] + padded[1:-1, 1:-1, :-2] - 2.0 * field
    return horizontal * lateral + vertical


def reference(fwd_prev, fwd_cur, bwd_next, bwd_cur, receiver_data, velocity_term, anisotropy, wavelet, shot_x, shot_y, aperture, snap_steps):
    horizontal = 1.0 + 2.0 * anisotropy
    surface = velocity_term[:, :, 0]
    slots = jnp.arange(NSNAP, dtype=jnp.int32)
    tile_of = (jnp.arange(NX, dtype=jnp.int32) // CX).astype(jnp.int32)
    half = SHOTS // 2

    def one_shot(image, shot):
        plane = ((jnp.arange(NX, dtype=jnp.int32) == shot_x[shot])[:, None] & (jnp.arange(NY, dtype=jnp.int32) == shot_y[shot])[None, :]).astype(jnp.float32)
        before = lax.dynamic_index_in_dim(fwd_prev, shot, 0, keepdims=False)
        current = lax.dynamic_index_in_dim(fwd_cur, shot, 0, keepdims=False)
        snaps = jnp.zeros((NSNAP, NX, NY, NZ), jnp.bfloat16)

        def record(snaps, field, time):
            is_hit = snap_steps == time
            found = jnp.any(is_hit)
            slot = jnp.sum(jnp.where(is_hit, slots, 0)).astype(jnp.int32)
            older = lax.dynamic_slice_in_dim(snaps, slot, 1, 0)
            newer = jnp.where(found, field.astype(jnp.bfloat16)[None], older)
            return lax.dynamic_update_slice_in_dim(snaps, newer, slot, 0)

        def forward_step(index, carry):
            before, current, snaps = carry
            snaps = record(snaps, current, index + 1)
            amplitude = wavelet[shot, index]
            after = 2.0 * current - before + velocity_term * laplace(current, horizontal)
            after = after.at[:, :, 0].add(surface * plane * amplitude)
            return current, after, snaps

        before, current, snaps = lax.fori_loop(0, STEPS - 1, forward_step, (before, current, snaps))
        snaps = record(snaps, current, STEPS)

        row = ((shot + half) % SHOTS).astype(jnp.int32)
        later = lax.dynamic_index_in_dim(bwd_next, row, 0, keepdims=False)
        wave = lax.dynamic_index_in_dim(bwd_cur, row, 0, keepdims=False)
        records = lax.dynamic_index_in_dim(receiver_data, row, 0, keepdims=False)

        def correlate(partial_value, field, time):
            is_hit = snap_steps == time
            found = jnp.any(is_hit)
            slot = jnp.sum(jnp.where(is_hit, slots, 0)).astype(jnp.int32)
            taken = lax.dynamic_index_in_dim(snaps, slot, 0, keepdims=False).astype(jnp.float32)
            return partial_value + jnp.where(found, taken * field, 0.0)

        def backward_step(index, carry):
            later, wave, partial_value = carry
            time = STEPS - index
            partial_value = correlate(partial_value, wave, time)
            trace = lax.dynamic_index_in_dim(records, time - 2, 0, keepdims=False)
            earlier = 2.0 * wave - later + velocity_term * laplace(wave, horizontal)
            earlier = earlier.at[:, :, 0].add(surface * trace)
            return wave, earlier, partial_value

        partial_value = jnp.zeros((NX, NY, NZ), jnp.float32)
        later, wave, partial_value = lax.fori_loop(0, STEPS - 1, backward_step, (later, wave, partial_value))
        partial_value = correlate(partial_value, wave, 1)
        inside = jnp.any(tile_of[:, None] == aperture[shot][None, :], axis=1).astype(jnp.float32)
        return image + partial_value * inside[:, None, None], None

    image, unused = lax.scan(one_shot, jnp.zeros((NX, NY, NZ), jnp.float32), jnp.arange(SHOTS, dtype=jnp.int32))
    return image
```

```python
import jax
import jax.numpy as jnp
from jax import lax
from jax.experimental import pallas as pl
from jax.experimental.pallas import tpu as pltpu
from jax.sharding import PartitionSpec as P


EDGE = 8
LANES = 128


def run_copies(copies):
    for copy in copies:
        copy.start()
    for copy in copies:
        copy.wait()


def fill_extended(dst, tile, left, right, sem, first, depth, rows, row_base, tile_rows):
    width = tile.shape[0]
    return [
        pltpu.make_async_copy(
            left, dst.at[pl.ds(first, depth), pl.ds(row_base, rows)], sem.at[0]
        ),
        pltpu.make_async_copy(
            tile.at[:, tile_rows] if tile_rows is not None else tile,
            dst.at[pl.ds(first + depth, width), pl.ds(row_base, rows)],
            sem.at[1],
        ),
        pltpu.make_async_copy(
            right, dst.at[pl.ds(first + depth + width, depth), pl.ds(row_base, rows)], sem.at[2]
        ),
    ]


def zero_edges(buf, rows):
    layers = buf.shape[0]
    zeros = jnp.zeros((layers, EDGE, LANES), jnp.float32)
    buf[:, 0:EDGE, :] = zeros
    buf[:, EDGE + rows : EDGE + rows + EDGE, :] = zeros


def scale_horizontal(vel, hor, lo, hi, rows, chunk):
    def body(x, carry):
        for r0 in range(0, rows, chunk):
            at = pl.ds(r0, chunk)
            hor[x, at, :] = vel[x, at, :] * (1.0 + 2.0 * hor[x, at, :])
        return carry

    lax.fori_loop(lo, hi, body, 0)


def stencil_step(src, dst, vel, hor, lo, hi, rows, chunk, top=None, shift=0):
    lane = lax.broadcasted_iota(jnp.int32, (chunk, LANES), 1)

    def body(x, carry):
        for r0 in range(0, rows, chunk):
            at = pl.ds(EDGE + r0, chunk)
            here = pl.ds(r0, chunk)
            c = src[x, at, :]
            lateral = src[x - 1, at, :] + src[x + 1, at, :]
            lateral = lateral + src[x, pl.ds(EDGE + r0 - 1, chunk), :]
            lateral = lateral + src[x, pl.ds(EDGE + r0 + 1, chunk), :]
            deeper = jnp.where(lane == LANES - 1, 0.0, pltpu.roll(c, LANES - 1, 1))
            if top is None:
                above = jnp.where(lane == 0, 0.0, pltpu.roll(c, 1, 1))
            else:
                data = top[x, here, :]
                if shift:
                    data = pltpu.roll(data, LANES - shift, 1)
                above = jnp.where(lane == 0, data, pltpu.roll(c, 1, 1))
            twice = c + c
            new = twice - dst[x, at, :]
            new = new + hor[x, here, :] * (lateral - (twice + twice))
            new = new + vel[x, here, :] * (deeper + above - twice)
            dst[x, at, :] = new
        return carry

    lax.fori_loop(lo, hi, body, 0)


def slot_of(steps, count, time):
    slot = jnp.int32(0)
    found = jnp.int32(0)
    for k in range(count):
        hit = (steps[k] == time).astype(jnp.int32)
        slot = slot + hit * k
        found = found + hit
    return slot, found > 0


def forward_call(cur, prev, vel, ani, halos, ints, amps, n_snaps, half_rows):
    width, rows, depth_cells = cur.shape
    reach = amps.shape[0]
    layers = width + 2 * reach
    chunk = 64
    cur_l, cur_r, prev_l, prev_r, vel_l, vel_r, ani_l, ani_r = halos

    def kernel(ints_ref, amps_ref, cur_t, cl, cr, prev_t, pl_, pr, vel_t, vl, vr, ani_t, al, ar,
               own_ref, send_ref, buf_a, buf_b, v_buf, h_buf, sem):
        near = reach - 1
        copies = fill_extended(v_buf, vel_t, vl, vr, sem.at[0], 1, near, rows, 0, None)
        copies += fill_extended(h_buf, ani_t, al, ar, sem.at[1], 1, near, rows, 0, None)
        copies += fill_extended(buf_a, cur_t, cl, cr, sem.at[2], 0, reach, rows, EDGE, None)
        copies += fill_extended(buf_b, prev_t, pl_, pr, sem.at[3], 1, near, rows, EDGE, None)
        for copy in copies:
            copy.start()
        zero_edges(buf_a, rows)
        zero_edges(buf_b, rows)
        for copy in copies[:6]:
            copy.wait()
        scale_horizontal(v_buf, h_buf, 1, layers - 1, rows, chunk)
        for copy in copies[6:]:
            copy.wait()
        steps = [ints_ref[k] for k in range(n_snaps)]
        source_x, source_y = ints_ref[n_snaps], ints_ref[n_snaps + 1]
        own_at, send_at = ints_ref[n_snaps + 2], ints_ref[n_snaps + 3]
        row8 = lax.broadcasted_iota(jnp.int32, (8, LANES), 0)
        lane8 = lax.broadcasted_iota(jnp.int32, (8, LANES), 1)

        def record(buf, time):
            slot, found = slot_of(steps, n_snaps, time)

            @pl.when(found)
            def _():
                def body(x, carry):
                    for r0 in range(0, half_rows, chunk):
                        for ref, at in ((own_ref, own_at), (send_ref, send_at)):
                            base = pl.multiple_of(EDGE + at + r0, 8)
                            ref[slot, x, pl.ds(r0, chunk), :] = buf[
                                reach + x, pl.ds(base, chunk), :
                            ].astype(jnp.bfloat16)
                    return carry

                lax.fori_loop(0, width, body, 0)

        src, dst = buf_a, buf_b
        record(src, 1)
        for step in range(1, reach + 1):
            lo, hi = step, layers - step
            stencil_step(src, dst, v_buf, h_buf, lo, hi, rows, chunk)

            @pl.when((source_x >= lo) & (source_x < hi))
            def _(dst=dst, step=step):
                base = pl.multiple_of((source_y // 8) * 8, 8)
                at = pl.ds(pl.multiple_of(base + EDGE, 8), 8)
                mask = (row8 == source_y - base) & (lane8 == 0)
                add = v_buf[source_x, pl.ds(base, 8), :] * amps_ref[step - 1]
                dst[source_x, at, :] = dst[source_x, at, :] + jnp.where(mask, add, 0.0)

            src, dst = dst, src
            record(src, step + 1)

    snaps = jax.ShapeDtypeStruct((n_snaps, width, half_rows, depth_cells), jnp.bfloat16)
    any_spec = pl.BlockSpec(memory_space=pl.ANY)
    smem = pl.BlockSpec(memory_space=pltpu.SMEM)
    vmem = pl.BlockSpec(memory_space=pltpu.VMEM)
    cells = layers * rows * depth_cells
    return pl.pallas_call(
        kernel,
        out_shape=(snaps, snaps),
        in_specs=[smem, smem] + [any_spec] * 12,
        out_specs=(vmem, vmem),
        scratch_shapes=[
            pltpu.VMEM((layers, rows + 2 * EDGE, depth_cells), jnp.float32),
            pltpu.VMEM((layers, rows + 2 * EDGE, depth_cells), jnp.float32),
            pltpu.VMEM((layers, rows, depth_cells), jnp.float32),
            pltpu.VMEM((layers, rows, depth_cells), jnp.float32),
            pltpu.SemaphoreType.DMA((4, 3)),
        ],
        cost_estimate=pl.CostEstimate(
            flops=15 * cells * reach, bytes_accessed=16 * cells, transcendentals=0
        ),
        name="forward_pass",
    )(ints, amps, cur, cur_l, cur_r, prev, prev_l, prev_r, vel, vel_l, vel_r, ani, ani_l, ani_r)


def backward_call(cur, nxt, vel, ani, top, halos, ints, reach, n_snaps, half_rows, snaps=None):
    width, in_rows, depth_cells = cur.shape
    rows = half_rows + EDGE
    layers = width + 2 * reach
    chunk = 88 if rows % 88 == 0 else EDGE
    cur_l, cur_r, nxt_l, nxt_r, vel_l, vel_r, ani_l, ani_r = halos
    out_chunk = 64

    def kernel(*refs):
        ints_ref = refs[0]
        (cur_t, cl, cr, nxt_t, nl, nr, vel_t, vl, vr, ani_t, al, ar, top_t) = refs[1:14]
        rest = refs[14:]
        if snaps is not None:
            snap_ref, rest = rest[0], rest[1:]
        out_ref, buf_a, buf_b, v_buf, h_buf, t_buf, sem = rest
        near = reach - 1
        steps = [ints_ref[k] for k in range(n_snaps)]
        first_row, skip, inside = ints_ref[n_snaps], ints_ref[n_snaps + 1], ints_ref[n_snaps + 2]
        window = pl.ds(pl.multiple_of(first_row, 8), rows)
        field_window = window if in_rows != rows else None

        def med(ref):
            return ref.at[:, window]

        copies = fill_extended(v_buf, vel_t, med(vl), med(vr), sem.at[0], 1, near, rows, 0, window)
        copies += fill_extended(h_buf, ani_t, med(al), med(ar), sem.at[1], 1, near, rows, 0, window)
        copies += fill_extended(buf_a, cur_t, cl, cr, sem.at[2], 0, reach, rows, EDGE, field_window)
        copies += fill_extended(buf_b, nxt_t, nl, nr, sem.at[3], 1, near, rows, EDGE, field_window)
        copies.append(
            pltpu.make_async_copy(top_t, t_buf.at[pl.ds(1, layers - 2)], sem.at[4, 0])
        )
        for copy in copies:
            copy.start()
        zero_edges(buf_a, rows)
        zero_edges(buf_b, rows)
        for copy in copies[:6]:
            copy.wait()
        scale_horizontal(v_buf, h_buf, 1, layers - 1, rows, chunk)
        for copy in copies[6:]:
            copy.wait()

        if snaps is not None:
            out_ref[...] = jnp.zeros_like(out_ref)

        def record(buf, time):
            slot, found = slot_of(steps, n_snaps, time)
            if snaps is not None:
                found = found & (inside > 0)

            @pl.when(found)
            def _():
                def body(x, carry):
                    for r0 in range(0, half_rows, out_chunk):
                        base = pl.multiple_of(EDGE + skip + r0, 8)
                        at = pl.ds(r0, out_chunk)
                        w = buf[reach + x, pl.ds(base, out_chunk), :]
                        if snaps is None:
                            out_ref[slot, x, at, :] = w
                        else:
                            u = snap_ref[slot, x, at, :].astype(jnp.float32)
                            out_ref[x, at, :] = out_ref[x, at, :] + u * w
                    return carry

                lax.fori_loop(0, width, body, 0)

        src, dst = buf_a, buf_b
        record(src, reach + 1)
        for step in range(1, reach + 1):
            stencil_step(
                src, dst, v_buf, h_buf, step, layers - step, rows, chunk, t_buf, reach - step
            )
            src, dst = dst, src
            record(src, reach + 1 - step)

    any_spec = pl.BlockSpec(memory_space=pl.ANY)
    smem = pl.BlockSpec(memory_space=pltpu.SMEM)
    vmem = pl.BlockSpec(memory_space=pltpu.VMEM)
    cells = layers * rows * depth_cells
    shape = (width, half_rows, depth_cells)
    if snaps is None:
        shape = (n_snaps,) + shape
    extra = [] if snaps is None else [snaps]
    return pl.pallas_call(
        kernel,
        out_shape=jax.ShapeDtypeStruct(shape, jnp.float32),
        in_specs=[smem] + [any_spec] * 13 + [vmem] * len(extra),
        out_specs=vmem,
        scratch_shapes=[
            pltpu.VMEM((layers, rows + 2 * EDGE, depth_cells), jnp.float32),
            pltpu.VMEM((layers, rows + 2 * EDGE, depth_cells), jnp.float32),
            pltpu.VMEM((layers, rows, depth_cells), jnp.float32),
            pltpu.VMEM((layers, rows, depth_cells), jnp.float32),
            pltpu.VMEM((layers, rows, depth_cells), jnp.float32),
            pltpu.SemaphoreType.DMA((5, 3)),
        ],
        cost_estimate=pl.CostEstimate(
            flops=15 * cells * reach, bytes_accessed=20 * cells, transcendentals=0
        ),
        name="backward_local" if snaps is None else "backward_imported",
    )(ints, cur, cur_l, cur_r, nxt, nxt_l, nxt_r, vel, vel_l, vel_r, ani, ani_l, ani_r, top, *extra)


def combine_call(arrived, waves, own, ints, groups):
    n_snaps, width, half_rows, depth_cells = waves.shape
    block = half_rows // groups

    def kernel(ints_ref, arrived_ref, waves_ref, own_ref, *outs):
        place, inside = ints_ref[0], ints_ref[1]
        for d, out in enumerate(outs):
            base = pl.multiple_of(lax.rem(place + d, groups) * block, 8)
            at = pl.ds(base, block)
            total = arrived_ref[0, 0, at, :].astype(jnp.float32) * waves_ref[0, 0, at, :]
            for k in range(1, n_snaps):
                total = total + arrived_ref[k, 0, at, :].astype(jnp.float32) * waves_ref[k, 0, at, :]
            out[0] = own_ref[0, at, :] + jnp.where(inside > 0, total, 0.0)

    out = jax.ShapeDtypeStruct((width, block, depth_cells), jnp.float32)
    piece = pl.BlockSpec((1, block, depth_cells), lambda x: (x, 0, 0))
    stack = pl.BlockSpec((n_snaps, 1, half_rows, depth_cells), lambda x: (0, x, 0, 0))
    return pl.pallas_call(
        kernel,
        grid=(width,),
        out_shape=(out,) * groups,
        in_specs=[
            pl.BlockSpec(memory_space=pltpu.SMEM),
            stack,
            stack,
            pl.BlockSpec((1, half_rows, depth_cells), lambda x: (x, 0, 0)),
        ],
        out_specs=(piece,) * groups,
        cost_estimate=pl.CostEstimate(
            flops=2 * waves.size, bytes_accessed=6 * waves.size, transcendentals=0
        ),
        name="combine",
    )(ints, arrived, waves, own)


def on_device(
    fwd_prev,
    fwd_cur,
    bwd_next,
    bwd_cur,
    receiver_data,
    velocity_term,
    anisotropy,
    wavelet,
    shot_x,
    shot_y,
    aperture,
    snap_steps,
):
    shots = lax.axis_size("shot")
    tiles = lax.axis_size("xy")
    me = lax.axis_index("shot")
    tile = lax.axis_index("xy")
    half = shots // 2
    side = me // half
    partner = (me + half) % shots
    width, rows = fwd_prev.shape[1], fwd_prev.shape[2]
    reach = wavelet.shape[1]
    near = reach - 1
    n_snaps = snap_steps.shape[0]
    half_rows = rows // 2
    cut_rows = half_rows + EDGE
    my_first = side * (half_rows - EDGE)
    their_first = (1 - side) * (half_rows - EDGE)
    across = [(i, (i + half) % shots) for i in range(shots)]
    up = [(i, i + 1) for i in range(tiles - 1)]
    down = [(i + 1, i) for i in range(tiles - 1)]

    def from_sides(x, depth):
        left = lax.ppermute(x[width - depth :], "xy", up)
        right = lax.ppermute(x[:depth], "xy", down)
        return left, right

    nxt, cur, data = bwd_next[0], bwd_cur[0], receiver_data[0]

    def cut(x, axis, first):
        return lax.dynamic_slice_in_dim(x, first, cut_rows, axis)

    there = tuple(
        lax.ppermute(cut(x, axis, their_first), "shot", across)
        for x, axis in ((cur, 1), (nxt, 1), (data, 2))
    )

    halos_u = from_sides(fwd_cur[0], reach) + from_sides(fwd_prev[0], near)
    halos_m = from_sides(velocity_term, near) + from_sides(anisotropy, near)

    chosen = (jnp.arange(shots, dtype=jnp.int32) == me).astype(jnp.int32)
    source_x = jnp.sum(chosen * shot_x) - tile * width + reach
    source_y = jnp.sum(chosen * shot_y)
    amps = jnp.sum(jnp.where(chosen[:, None] > 0, wavelet, 0.0), axis=0)

    def inside_of(shot):
        mine = (jnp.arange(shots, dtype=jnp.int32) == shot)[:, None] & (aperture == tile)
        return jnp.any(mine).astype(jnp.int32)

    ints_u = jnp.concatenate(
        [snap_steps, jnp.stack([source_x, source_y, side * half_rows, (1 - side) * half_rows])]
    ).astype(jnp.int32)
    own, sent = forward_call(
        fwd_cur[0], fwd_prev[0], velocity_term, anisotropy, halos_u + halos_m, ints_u, amps,
        n_snaps, half_rows,
    )

    def surface_stack(x):
        left = lax.ppermute(x[:, width - near :], "xy", up)
        right = lax.ppermute(x[:, :near], "xy", down)
        wide = jnp.concatenate([left, x, right], axis=1)
        return jnp.pad(jnp.transpose(wide, (1, 2, 0)), ((0, 0), (0, 0), (0, LANES - reach)))

    def backward(cur, nxt, data, cut_cur, cut_nxt, inside, snaps):
        halos = from_sides(cut_cur, reach) + from_sides(cut_nxt, near)
        ints = jnp.concatenate(
            [snap_steps, jnp.stack([my_first, side * EDGE, inside])]
        ).astype(jnp.int32)
        return backward_call(
            cur, nxt, velocity_term, anisotropy, surface_stack(data), halos + halos_m, ints,
            reach, n_snaps, half_rows, snaps,
        )

    waves = backward(
        cur, nxt, cut(data, 2, my_first), cut(cur, 1, my_first), cut(nxt, 1, my_first),
        jnp.int32(1), None,
    )
    sent, there = lax.optimization_barrier((sent, there))
    arrived = lax.ppermute(sent, "shot", across)
    there_cur, there_nxt, there_data = there
    own_image = backward(
        there_cur, there_nxt, there_data, there_cur, there_nxt, inside_of(me), own
    )
    place = me % half
    blocks = combine_call(
        arrived, waves, own_image, jnp.stack([place, inside_of(partner)]).astype(jnp.int32), half
    )
    total = blocks[0]
    for d in range(1, half):
        route = [(i, (i // half) * half + (i % half + d) % half) for i in range(shots)]
        total = total + lax.ppermute(blocks[d], "shot", route)
    return total


def solution(mesh):
    in_specs = (
        P("shot", "xy", None, None),
        P("shot", "xy", None, None),
        P("shot", "xy", None, None),
        P("shot", "xy", None, None),
        P("shot", None, "xy", None),
        P("xy", None, None),
        P("xy", None, None),
        P(),
        P(),
        P(),
        P(),
        P(),
    )
    out_specs = P("xy", "shot", None)
    return jax.shard_map(
        on_device, mesh=mesh, in_specs=in_specs, out_specs=out_specs, check_vma=False
    )
```

```python
import jax
import jax.numpy as jnp
from jax import lax
from jax.experimental import pallas as pl
from jax.experimental.pallas import tpu as pltpu
from jax.sharding import PartitionSpec as P


PAD = 8
EDGE = 16
LANES = 128
WIRE = jnp.int16
STEPS_OF_SCALE = (32, 16, 8, 4, 2, 1)
FIXED = 65536.0


def spans(rows, chunk):
    return [(r0, min(chunk, rows - r0)) for r0 in range(0, rows, chunk)]


def neighbour_matrix():
    row = lax.broadcasted_iota(jnp.int32, (2 * LANES, LANES), 0)
    column = lax.broadcasted_iota(jnp.int32, (2 * LANES, LANES), 1)
    row = jnp.where(row >= LANES, row - LANES, row)
    beside = (row - column == 1) | (column - row == 1)
    return jnp.where(beside, 1.0, 0.0).astype(jnp.bfloat16)


def stencil_step(src, dst, coefs, lo, hi, rows, beside, sums, surface=None):
    centre, hor, vel = coefs

    def body(i, carry):
        x = lo + 2 * i
        for j in range(2):
            for r0, size in spans(rows, 144):
                c = src[x + j, pl.ds(PAD + r0, size), :]
                high = c.astype(jnp.bfloat16)
                low = (c - high.astype(jnp.float32)).astype(jnp.bfloat16)
                sums[j, pl.ds(r0, size), :] = jnp.dot(
                    jnp.concatenate([high, low], axis=1), beside[...],
                    preferred_element_type=jnp.float32,
                )
        shifts = [None, None] if surface is None else [surface[1](x), surface[1](x + 1)]
        for r0, size in spans(rows, 32):
            at = pl.ds(PAD + r0, size)
            here = pl.ds(r0, size)
            c = [src[x - 1 + j, at, :] for j in range(4)]
            for j in range(2):
                mid = c[j + 1]
                lateral = c[j] + c[j + 2]
                lateral = lateral + src[x + j, pl.ds(PAD + r0 - 1, size), :]
                lateral = lateral + src[x + j, pl.ds(PAD + r0 + 1, size), :]
                vertical = sums[j, here, :]
                if surface is not None:
                    lane = lax.broadcasted_iota(jnp.int32, (size, LANES), 1)
                    plane, shift = shifts[j]
                    data = pltpu.roll(surface[0][plane, here, :], shift, 1)
                    vertical = vertical + jnp.where(lane == 0, data, 0.0)
                new = centre[x + j, here, :] * mid - dst[x + j, at, :]
                new = new + hor[x + j, here, :] * lateral
                new = new + vel[x + j, here, :] * vertical
                dst[x + j, at, :] = new
        return carry

    lax.fori_loop(0, (hi - lo) // 2, body, 0)


def header_rows(first, half_rows):
    return jnp.where(first == 0, half_rows + 8, 0)


def encode_scale(top):
    up, down, exponent = jnp.ones_like(top), jnp.ones_like(top), jnp.zeros_like(top)
    for j in STEPS_OF_SCALE:
        more = top * 2.0**j
        fits = more < 15.9
        top = jnp.where(fits, more, top)
        up = jnp.where(fits, up * 2.0**j, up)
        down = jnp.where(fits, down * 2.0**-j, down)
        exponent = jnp.where(fits, exponent + j, exponent)
    return up * 2048.0, down / 2048.0, exponent


def decode_scale(stage, layer, first, half_rows):
    base = pl.multiple_of(jnp.where(first == 0, half_rows, 0), 16)
    block = stage[layer, pl.ds(base, 16), :].astype(jnp.int32).astype(jnp.float32)
    row = lax.broadcasted_iota(jnp.int32, (16, LANES), 0)
    skip = jnp.where(first == 0, 8, 0)
    held = (row >= skip) & (row < skip + 8)
    exponent = jnp.max(jnp.where(held, block, 0.0), axis=(0, 1), keepdims=True)
    scale = jnp.full_like(exponent, 1.0 / 2048.0)
    for j in STEPS_OF_SCALE:
        holds = exponent >= j
        scale = jnp.where(holds, scale * 2.0**-j, scale)
        exponent = jnp.where(holds, exponent - j, exponent)
    return scale


def slot_of(steps, time):
    slot = jnp.int32(0)
    found = jnp.int32(0)
    for k, step in enumerate(steps):
        hit = (step == time).astype(jnp.int32)
        slot = slot + hit * k
        found = found + hit
    return slot, found > 0


def wave_pass(kind, field, field_at, vel, ani, left, right, halo_at, ints, amps, half_rows, reach,
              n_snaps, blocks=1, others=(), data=None):
    width, all_rows, depth_cells = vel.shape
    rows = half_rows + EDGE
    layers = width + 2 * reach
    near = reach - 1
    backward = kind in ("waves", "image")
    packed = not isinstance(field, tuple)
    fields = [field] if packed else list(field) + ([data] if backward else [])
    depths = (reach, near, near, near) + ((1,) if backward else ())
    n_side = len(left)

    def kernel(*refs):
        ints_ref, amps_ref = refs[0], refs[1]
        pos = 2
        field_refs = refs[pos : pos + len(fields)]
        pos += len(fields)
        vel_ref, ani_ref = refs[pos : pos + 2]
        pos += 2
        left_refs = refs[pos : pos + n_side]
        pos += n_side
        right_refs = refs[pos : pos + n_side]
        pos += n_side
        other_hbm = refs[pos : pos + len(others)]
        pos += len(others)
        n_out = blocks if kind == "blocks" else 1
        outs = refs[pos : pos + n_out]
        pos += n_out
        buf_a, buf_b, v_buf, h_buf, c_buf, stage_l, stage_r, stage_t, top, beside, sums, sem = refs[
            pos : pos + 12
        ]

        steps = [ints_ref[k] for k in range(n_snaps)]
        first_row, skip, inside, source_x, source_y, place = [
            ints_ref[n_snaps + k] for k in range(6)
        ]
        window = pl.ds(pl.multiple_of(first_row, 8), rows)
        inner = pl.ds(PAD, rows)

        tile_copies = [
            pltpu.make_async_copy(
                vel_ref.at[:, window], v_buf.at[pl.ds(reach, width)], sem.at[0]
            ),
            pltpu.make_async_copy(
                ani_ref.at[:, window], h_buf.at[pl.ds(reach, width)], sem.at[1]
            ),
        ]
        side_copies = []
        where = 0
        offsets = []
        for depth, (pack, layer) in zip(depths, halo_at):
            n = len(side_copies)
            side_copies.append(
                pltpu.make_async_copy(
                    left_refs[pack].at[pl.ds(layer, depth)],
                    stage_l.at[pl.ds(where, depth)],
                    sem.at[2 + n],
                )
            )
            side_copies.append(
                pltpu.make_async_copy(
                    right_refs[pack].at[pl.ds(layer, depth)],
                    stage_r.at[pl.ds(where, depth)],
                    sem.at[3 + n],
                )
            )
            offsets.append(where)
            where += depth
        if packed:
            field_copies = [pltpu.make_async_copy(field_refs[0], stage_t, sem.at[12])]
        else:
            field_copies = [
                pltpu.make_async_copy(
                    field_refs[0].at[:, window], buf_a.at[pl.ds(reach, width), inner], sem.at[12]
                ),
                pltpu.make_async_copy(
                    field_refs[1].at[:, window], buf_b.at[pl.ds(reach, width), inner], sem.at[13]
                ),
            ]
            if backward:
                n_data = data.shape[0]
                flat = refs[-2]
                field_copies.append(
                    pltpu.make_async_copy(field_refs[2], flat.at[pl.ds(0, n_data)], sem.at[14])
                )
                flat[n_data:, :] = jnp.zeros((LANES - n_data, all_rows), jnp.float32)
        other_refs = refs[pos + 12 : pos + 12 + len(others)]
        other_copies = [
            pltpu.make_async_copy(source, target, sem.at[15 + n])
            for n, (source, target) in enumerate(zip(other_hbm, other_refs))
        ]
        for copy in tile_copies + side_copies + field_copies + other_copies:
            copy.start()
        beside[...] = neighbour_matrix()
        zeros = jnp.zeros((layers, PAD, LANES), jnp.float32)
        for buf in (buf_a, buf_b):
            buf[:, 0:PAD, :] = zeros
            buf[:, PAD + rows : PAD + rows + PAD, :] = zeros
        for copy in side_copies:
            copy.wait()

        def widen(stage, at, dst, first, count, row0, scale):
            def body(x, carry):
                for r0, size in spans(rows, 64):
                    code = stage[at + x, pl.ds(r0, size), :].astype(jnp.int32)
                    dst[first + x, pl.ds(row0 + r0, size), :] = code.astype(jnp.float32) * scale
                return carry

            lax.fori_loop(0, count, body, 0)

        side_scales = []
        for stage, starts in ((stage_l, (0, 1, 1, 1)), (stage_r, (reach + width,) * 4)):
            scale = decode_scale(stage, offsets[0], first_row, half_rows)
            side_scales.append(scale)
            for dst, at, start, depth, row0, unit in zip(
                (buf_a, buf_b, v_buf, h_buf), offsets, starts, depths, (PAD, PAD, 0, 0),
                (scale, scale, 1.0 / FIXED, 1.0 / FIXED),
            ):
                widen(stage, at, dst, start, depth, row0, unit)
        for copy in tile_copies:
            copy.wait()

        def coefficients(x, carry):
            for r0, size in spans(rows, 64):
                at = pl.ds(r0, size)
                v = v_buf[x, at, :]
                h = v * (1.0 + 2.0 * h_buf[x, at, :])
                h_buf[x, at, :] = h
                c_buf[x, at, :] = 2.0 - (4.0 * h + 2.0 * v)
            return carry

        lax.fori_loop(1, layers - 1, coefficients, 0)
        for copy in field_copies:
            copy.wait()
        if packed:
            scale = decode_scale(stage_t, field_at[0], first_row, half_rows)
            widen(stage_t, field_at[0], buf_a, reach, width, PAD, scale)
            widen(stage_t, field_at[1], buf_b, reach, width, PAD, scale)
        surface = None
        if backward:
            widen(stage_l, offsets[4], top, 0, 1, 0, side_scales[0])
            if packed:
                widen(stage_t, field_at[2], top, 1, 1, 0, scale)
            else:
                turned = refs[-1]
                turned[...] = flat[...].T
                top[1] = turned[window, :]
            widen(stage_r, offsets[4], top, 2, 1, 0, side_scales[1])

        if kind in ("image", "blocks"):
            image = outs[0] if kind == "image" else refs[-1]
            image[...] = jnp.zeros_like(image)

        def record(buf, time):
            slot, found = slot_of(steps, time)
            if kind in ("image", "blocks"):
                found = found & (inside > 0)

            @pl.when(found)
            def _():
                def body(x, carry):
                    for r0, size in spans(half_rows, 64):
                        base = pl.multiple_of(PAD + skip + r0, 8)
                        at = pl.ds(r0, size)
                        value = buf[reach + x, pl.ds(base, size), :]
                        if kind in ("snaps", "waves"):
                            outs[0][slot, x, at, :] = value.astype(outs[0].dtype)
                        elif kind == "image":
                            u = other_refs[0][slot, x, at, :].astype(jnp.float32)
                            image[x, at, :] = image[x, at, :] + u * value
                        else:
                            u = value.astype(jnp.bfloat16).astype(jnp.float32)
                            image[x, at, :] = image[x, at, :] + u * other_refs[1][slot, x, at, :]
                    return carry

                lax.fori_loop(0, width, body, 0)

        src, dst = buf_a, buf_b
        coefs = (c_buf, h_buf, v_buf)
        for copy in other_copies:
            copy.wait()
        record(src, reach + 1 if backward else 1)
        for step in range(1, reach + 1):
            lo, hi = step, layers - step
            if backward:

                def shift(x, step=step):
                    past = x - reach + width
                    plane = past // width
                    lane = (reach - step) * width + past - plane * width
                    return plane, lax.rem(LANES - lane, LANES)

                surface = (top, shift)
            stencil_step(src, dst, coefs, lo, hi, rows, beside, sums, surface)
            if not backward:
                row8 = lax.broadcasted_iota(jnp.int32, (8, LANES), 0)
                lane8 = lax.broadcasted_iota(jnp.int32, (8, LANES), 1)

                @pl.when((source_x >= lo) & (source_x < hi) & (source_y >= 0) & (source_y < rows))
                def _(dst=dst, step=step):
                    base = pl.multiple_of((source_y // 8) * 8, 8)
                    at = pl.ds(pl.multiple_of(base + PAD, 8), 8)
                    mask = (row8 == source_y - base) & (lane8 == 0)
                    add = v_buf[source_x, pl.ds(base, 8), :] * amps_ref[step - 1]
                    dst[source_x, at, :] = dst[source_x, at, :] + jnp.where(mask, add, 0.0)

            src, dst = dst, src
            record(src, reach + 1 - step if backward else step + 1)

        if kind == "blocks":
            block = half_rows // blocks
            for d, out in enumerate(outs):
                base = pl.multiple_of(lax.rem(place + d, blocks) * block, 8)

                def cut(x, carry, out=out, base=base):
                    at = pl.ds(base, block)
                    out[x] = other_refs[0][x, at, :] + image[x, at, :]
                    return carry

                lax.fori_loop(0, width, cut, 0)

    any_spec = pl.BlockSpec(memory_space=pl.ANY)
    smem = pl.BlockSpec(memory_space=pltpu.SMEM)
    vmem = pl.BlockSpec(memory_space=pltpu.VMEM)
    shape = (width, half_rows, depth_cells)
    if kind == "blocks":
        out_shape = (jax.ShapeDtypeStruct((width, half_rows // blocks, depth_cells), jnp.float32),) * blocks
    elif kind == "image":
        out_shape = (jax.ShapeDtypeStruct(shape, jnp.float32),)
    else:
        dtype = jnp.bfloat16 if kind == "snaps" else jnp.float32
        out_shape = (jax.ShapeDtypeStruct((n_snaps,) + shape, dtype),)
    cells = layers * rows * depth_cells
    grid_buf = pltpu.VMEM((layers, rows, depth_cells), jnp.float32)
    field_buf = pltpu.VMEM((layers, rows + 2 * PAD, depth_cells), jnp.float32)
    stage_layers = field.shape[0] if packed else 1
    side = pltpu.VMEM((sum(depths), rows, depth_cells), WIRE)
    return pl.pallas_call(
        kernel,
        out_shape=out_shape,
        in_specs=[smem, smem] + [any_spec] * (len(fields) + 2 + 2 * n_side + len(others)),
        out_specs=(vmem,) * len(out_shape),
        scratch_shapes=[
            field_buf, field_buf, grid_buf, grid_buf, grid_buf, side, side,
            pltpu.VMEM((stage_layers, rows, depth_cells), WIRE),
            pltpu.VMEM((3, rows, depth_cells), jnp.float32),
            pltpu.VMEM((2 * LANES, LANES), jnp.bfloat16),
            pltpu.VMEM((2, rows, depth_cells), jnp.float32),
            pltpu.SemaphoreType.DMA((18,)),
        ]
        + [pltpu.VMEM(other.shape, other.dtype) for other in others]
        + ([pltpu.VMEM(shape, jnp.float32)] if kind == "blocks" else [])
        + (
            [pltpu.VMEM((LANES, all_rows), jnp.float32), pltpu.VMEM((all_rows, LANES), jnp.float32)]
            if kind == "waves"
            else []
        ),
        cost_estimate=pl.CostEstimate(
            flops=15 * cells * reach, bytes_accessed=20 * cells, transcendentals=0
        ),
    )(ints, amps, *fields, vel, ani, *left, *right, *others)


def any_specs(n):
    return [pl.BlockSpec(memory_space=pl.ANY)] * n


def pack_rows(first, fields, ranges, groups, data):
    width, all_rows, depth_cells = fields[0].shape
    half_rows = all_rows // 2
    rows = half_rows + EDGE
    tail = 0 if data is None else 1
    sizes = [sum(hi - lo for _, lo, hi in r) + tail for r in ranges]
    n = len(fields)
    loose = [i for i in range(n) if not any(i in group for group in groups)]

    def kernel(first_ref, *refs):
        field_refs = refs[:n]
        outs = refs[n + tail : n + tail + len(ranges)]
        rest = refs[n + tail + len(ranges) :]
        wide, narrow, sem, out_sem = rest[:4]
        window = pl.ds(pl.multiple_of(first_ref[0], 16), rows)
        spare = pl.ds(pl.multiple_of(header_rows(first_ref[0], half_rows), 8), 8)
        copies = [
            pltpu.make_async_copy(ref.at[:, window], wide.at[i], sem.at[i])
            for i, ref in enumerate(field_refs)
        ]
        for copy in copies:
            copy.start()
        started = []

        def go(source, target):
            copy = pltpu.make_async_copy(source, target, out_sem.at[len(started)])
            copy.start()
            started.append(copy)

        def code(values, scale):
            return jnp.floor(values * scale + 0.5).astype(jnp.int32).astype(WIRE)

        def put(i, scale):
            def body(x, carry):
                for r0, size in spans(rows, 64):
                    at = pl.ds(r0, size)
                    narrow[i, x, at, :] = code(wide[i, x, at, :], scale)
                return carry

            lax.fori_loop(0, width, body, 0)
            for out, pieces in zip(outs, ranges):
                where = 0
                for field, lo, hi in pieces:
                    if field == i:
                        go(narrow.at[i, pl.ds(lo, hi - lo)], out.at[pl.ds(where, hi - lo)])
                    where += hi - lo

        for number, group in enumerate(groups):
            with_data = tail and number == len(groups) - 1
            if with_data:
                flat, turned = rest[4:6]
                load = pltpu.make_async_copy(refs[n], flat.at[pl.ds(0, data.shape[0])], sem.at[n])
                load.start()
                load.wait()
                flat[data.shape[0] :, :] = jnp.zeros((LANES - data.shape[0], all_rows), jnp.float32)
                turned[...] = flat[...].T
            top = jnp.zeros((8, LANES), jnp.float32)
            for i in group:
                copies[i].wait()

                def largest(x, top, i=i):
                    for r0, size in spans(rows, 64):
                        block = jnp.abs(wide[i, x, pl.ds(r0, size), :])
                        top = jnp.maximum(top, jnp.max(block.reshape(-1, 8, LANES), axis=0))
                    return top

                top = lax.fori_loop(0, width, largest, top)
            if with_data:
                block = jnp.abs(turned[window, :])
                top = jnp.maximum(top, jnp.max(block.reshape(-1, 8, LANES), axis=0))
            top = jnp.max(top, axis=(0, 1), keepdims=True)
            scale, unit, exponent = encode_scale(top)
            header = jnp.broadcast_to(exponent * unit, (8, LANES))
            for x in range(width):
                wide[group[0], x, spare, :] = header
            for i in group:
                put(i, scale)
            if with_data:
                narrow[n, 0] = code(turned[window, :], scale)
                for out, size in zip(outs, sizes):
                    go(narrow.at[n, pl.ds(0, 1)], out.at[pl.ds(size - 1, 1)])
        for i in loose:
            copies[i].wait()
            put(i, FIXED)
        for copy in started:
            copy.wait()

    n_out = sum(len(r) for r in ranges) + tail * len(ranges)
    scratch = [
        pltpu.VMEM((n, width, rows, depth_cells), jnp.float32),
        pltpu.VMEM((n + tail, width, rows, depth_cells), WIRE),
        pltpu.SemaphoreType.DMA((n + 1,)),
        pltpu.SemaphoreType.DMA((n_out,)),
    ]
    if tail:
        scratch += [
            pltpu.VMEM((LANES, all_rows), jnp.float32),
            pltpu.VMEM((all_rows, LANES), jnp.float32),
        ]
    cells = n * width * rows * depth_cells
    return pl.pallas_call(
        kernel,
        out_shape=tuple(jax.ShapeDtypeStruct((m, rows, depth_cells), WIRE) for m in sizes),
        in_specs=[pl.BlockSpec(memory_space=pltpu.SMEM)] + any_specs(n + tail),
        out_specs=tuple(any_specs(len(sizes))),
        scratch_shapes=scratch,
        cost_estimate=pl.CostEstimate(flops=cells, bytes_accessed=8 * cells, transcendentals=0),
        name="pack_rows",
    )(first, *fields, *([] if data is None else [data]))


def repack(packed, ranges):
    sizes = [sum(hi - lo for lo, hi in r) for r in ranges]
    n_out = sum(len(r) for r in ranges)

    def kernel(packed_ref, *refs):
        outs = refs[: len(ranges)]
        stage, sem, out_sem = refs[len(ranges) :]
        load = pltpu.make_async_copy(packed_ref, stage, sem.at[0])
        load.start()
        load.wait()
        started = []
        for out, pieces in zip(outs, ranges):
            where = 0
            for lo, hi in pieces:
                copy = pltpu.make_async_copy(
                    stage.at[pl.ds(lo, hi - lo)],
                    out.at[pl.ds(where, hi - lo)],
                    out_sem.at[len(started)],
                )
                copy.start()
                started.append(copy)
                where += hi - lo
        for copy in started:
            copy.wait()

    return pl.pallas_call(
        kernel,
        out_shape=tuple(jax.ShapeDtypeStruct((m,) + packed.shape[1:], packed.dtype) for m in sizes),
        in_specs=any_specs(1),
        out_specs=tuple(any_specs(len(sizes))),
        scratch_shapes=[
            pltpu.VMEM(packed.shape, packed.dtype),
            pltpu.SemaphoreType.DMA((1,)),
            pltpu.SemaphoreType.DMA((n_out,)),
        ],
        cost_estimate=pl.CostEstimate(
            flops=0, bytes_accessed=6 * packed.size, transcendentals=0
        ),
        name="repack",
    )(packed)


def on_device(
    fwd_prev,
    fwd_cur,
    bwd_next,
    bwd_cur,
    receiver_data,
    velocity_term,
    anisotropy,
    wavelet,
    shot_x,
    shot_y,
    aperture,
    snap_steps,
):
    shots = lax.axis_size("shot")
    tiles = lax.axis_size("xy")
    me = lax.axis_index("shot")
    tile = lax.axis_index("xy")
    half = shots // 2
    side = me // half
    partner = (me + half) % shots
    width, rows = fwd_prev.shape[1], fwd_prev.shape[2]
    reach = wavelet.shape[1]
    near = reach - 1
    n_snaps = snap_steps.shape[0]
    half_rows = rows // 2
    my_first = side * (half_rows - EDGE)
    their_first = (1 - side) * (half_rows - EDGE)
    across = [(i, (i + half) % shots) for i in range(shots)]
    up = [(i, i + 1) for i in range(tiles - 1)]
    down = [(i + 1, i) for i in range(tiles - 1)]
    u0, u1, w9, w8 = fwd_prev[0], fwd_cur[0], bwd_next[0], bwd_cur[0]

    data = receiver_data[0].reshape(reach * width, rows)

    def at(first):
        return jnp.reshape(first, (1,)).astype(jnp.int32)

    whole = ((0, 0, width), (1, 0, width))
    (send_w,) = pack_rows(at(their_first), (w8, w9), (whole,), ((0, 1),), data)
    import_w = lax.ppermute(send_w, "shot", across)
    (send_u,) = pack_rows(at(their_first), (u1, u0), (whole,), ((0, 1),), None)
    import_u = lax.ppermute(send_u, "shot", across)

    local = (u1, u0, velocity_term, anisotropy, w8, w9)
    depths = (reach, near, near, near, reach, near)
    up_m, down_m = pack_rows(
        at(my_first), local,
        (
            [(i, width - d, width) for i, d in enumerate(depths)],
            [(i, 0, d) for i, d in enumerate(depths)],
        ),
        ((0, 1), (4, 5)), data,
    )
    left = lax.ppermute(up_m, "xy", up)
    right = lax.ppermute(down_m, "xy", down)

    def numbers(shot):
        chosen = (jnp.arange(shots, dtype=jnp.int32) == shot).astype(jnp.int32)
        source_x = jnp.sum(chosen * shot_x) - tile * width + reach
        source_y = jnp.sum(chosen * shot_y) - my_first
        inside = jnp.any((chosen[:, None] > 0) & (aperture == tile)).astype(jnp.int32)
        amps = jnp.sum(jnp.where(chosen[:, None] > 0, wavelet, 0.0), axis=0)
        parts = jnp.stack([my_first, side * EDGE, inside, source_x, source_y, me % half])
        return jnp.concatenate([snap_steps, parts]).astype(jnp.int32), amps

    ints_me, amps_me = numbers(me)
    ints_partner, amps_partner = numbers(partner)
    common = dict(half_rows=half_rows, reach=reach, n_snaps=n_snaps)
    at_v, at_a = (0, reach + near), (0, reach + 2 * near)
    at_w = reach + 3 * near
    (snaps,) = wave_pass(
        "snaps", (u1, u0), None, velocity_term, anisotropy, [left], [right],
        ((0, 0), (0, reach), at_v, at_a), ints_me, amps_me, **common,
    )

    def from_sides(packed, tail):
        ends = [(2 * width, 2 * width + 1)] if tail else []
        send_up, send_down = repack(
            packed,
            (
                [(width - reach, width), (2 * width - near, 2 * width)] + ends,
                [(0, reach), (width, width + near)] + ends,
            ),
        )
        from_left = lax.ppermute(send_up, "xy", up)
        from_right = lax.ppermute(send_down, "xy", down)
        return from_left, from_right

    (waves,) = wave_pass(
        "waves", (w8, w9), None, velocity_term, anisotropy, [left], [right],
        ((0, at_w), (0, at_w + reach), at_v, at_a, (0, at_w + reach + near)),
        ints_partner, amps_partner, data=data, **common,
    )
    left_w, right_w = from_sides(import_w, True)
    (image,) = wave_pass(
        "image", import_w, (0, width, 2 * width), velocity_term, anisotropy,
        [left, left_w], [right, right_w],
        ((1, 0), (1, reach), at_v, at_a, (1, reach + near)),
        ints_me, amps_me, others=(snaps,), **common,
    )
    left_u, right_u = from_sides(import_u, False)
    blocks = wave_pass(
        "blocks", import_u, (0, width), velocity_term, anisotropy,
        [left, left_u], [right, right_u], ((1, 0), (1, reach), at_v, at_a),
        ints_partner, amps_partner, blocks=half, others=(image, waves), **common,
    )
    total = blocks[0]
    for d in range(1, half):
        route = [(i, (i // half) * half + (i % half + d) % half) for i in range(shots)]
        arrived = lax.ppermute(blocks[d], "shot", route)
        total = total + arrived
    return total


def solution(mesh):
    in_specs = (
        P("shot", "xy", None, None),
        P("shot", "xy", None, None),
        P("shot", "xy", None, None),
        P("shot", "xy", None, None),
        P("shot", None, "xy", None),
        P("xy", None, None),
        P("xy", None, None),
        P(),
        P(),
        P(),
        P(),
        P(),
    )
    out_specs = P("xy", "shot", None)

    return jax.shard_map(
        on_device, mesh=mesh, in_specs=in_specs, out_specs=out_specs, check_vma=False
    )
```

```python
import jax
import jax.numpy as jnp
from jax import lax
from jax.experimental import pallas as pl
from jax.experimental.pallas import tpu as pltpu
from jax.sharding import PartitionSpec as P


PAD = 8
EDGE = 16
LANES = 128
WIRE = jnp.int16
STEPS_OF_SCALE = (32, 16, 8, 4, 2, 1)
FIXED = 65536.0


def spans(rows, chunk):
    return [(r0, min(chunk, rows - r0)) for r0 in range(0, rows, chunk)]


def neighbour_matrix():
    row = lax.broadcasted_iota(jnp.int32, (2 * LANES, LANES), 0)
    column = lax.broadcasted_iota(jnp.int32, (2 * LANES, LANES), 1)
    row = jnp.where(row >= LANES, row - LANES, row)
    beside = (row - column == 1) | (column - row == 1)
    return jnp.where(beside, 1.0, 0.0).astype(jnp.bfloat16)


def stencil_step(src, dst, coefs, lo, hi, rows, beside, sums, surface=None):
    centre, hor, vel = coefs

    def vertical_sums(x, j):
        for r0, size in spans(rows, 144):
            c = src[x, pl.ds(PAD + r0, size), :]
            high = c.astype(jnp.bfloat16)
            low = (c - high.astype(jnp.float32)).astype(jnp.bfloat16)
            sums[j, pl.ds(r0, size), :] = jnp.dot(
                jnp.concatenate([high, low], axis=1), beside[...],
                preferred_element_type=jnp.float32,
            )

    def one_layer(x, j):
        for r0, size in spans(rows, 32):
            at = pl.ds(PAD + r0, size)
            here = pl.ds(r0, size)
            lateral = src[x - 1, at, :] + src[x + 1, at, :]
            lateral = lateral + src[x, pl.ds(PAD + r0 - 1, size), :]
            lateral = lateral + src[x, pl.ds(PAD + r0 + 1, size), :]
            vertical = sums[j, here, :]
            if surface is not None:
                lane = lax.broadcasted_iota(jnp.int32, (size, LANES), 1)
                plane, shift = surface[1](x)
                data = pltpu.roll(surface[0][plane, here, :], shift, 1)
                vertical = vertical + jnp.where(lane == 0, data, 0.0)
            new = centre[x, here, :] * src[x, at, :] - dst[x, at, :]
            new = new + hor[x, here, :] * lateral
            new = new + vel[x, here, :] * vertical
            dst[x, at, :] = new

    def body(i, carry):
        x = lo + 2 * i
        vertical_sums(x + 1, 1)
        one_layer(x, 0)
        vertical_sums(x + 2, 0)
        one_layer(x + 1, 1)
        return carry

    vertical_sums(lo, 0)
    lax.fori_loop(0, (hi - lo) // 2, body, 0)


def header_rows(first, half_rows):
    return jnp.where(first == 0, half_rows + 8, 0)


def encode_scale(top):
    up, down, exponent = jnp.ones_like(top), jnp.ones_like(top), jnp.zeros_like(top)
    for j in STEPS_OF_SCALE:
        more = top * 2.0**j
        fits = more < 15.9
        top = jnp.where(fits, more, top)
        up = jnp.where(fits, up * 2.0**j, up)
        down = jnp.where(fits, down * 2.0**-j, down)
        exponent = jnp.where(fits, exponent + j, exponent)
    return up * 2048.0, down / 2048.0, exponent


def decode_scale(stage, layer, first, half_rows):
    base = pl.multiple_of(jnp.where(first == 0, half_rows, 0), 16)
    block = stage[layer, pl.ds(base, 16), :].astype(jnp.int32).astype(jnp.float32)
    row = lax.broadcasted_iota(jnp.int32, (16, LANES), 0)
    skip = jnp.where(first == 0, 8, 0)
    held = (row >= skip) & (row < skip + 8)
    exponent = jnp.max(jnp.where(held, block, 0.0), axis=(0, 1), keepdims=True)
    scale = jnp.full_like(exponent, 1.0 / 2048.0)
    for j in STEPS_OF_SCALE:
        holds = exponent >= j
        scale = jnp.where(holds, scale * 2.0**-j, scale)
        exponent = jnp.where(holds, exponent - j, exponent)
    return scale


def slot_of(steps, time):
    slot = jnp.int32(0)
    found = jnp.int32(0)
    for k, step in enumerate(steps):
        hit = (step == time).astype(jnp.int32)
        slot = slot + hit * k
        found = found + hit
    return slot, found > 0


def wave_pass(kind, field, field_at, vel, ani, left, right, halo_at, ints, amps, half_rows, reach,
              n_snaps, blocks=1, others=(), data=None):
    width, all_rows, depth_cells = vel.shape
    rows = half_rows + EDGE
    layers = width + 2 * reach
    near = reach - 1
    backward = kind in ("waves", "image")
    packed = not isinstance(field, tuple)
    fields = [field] if packed else list(field) + ([data] if backward else [])
    depths = (reach, near, near, near) + ((1,) if backward else ())
    n_side = len(left)

    def kernel(*refs):
        ints_ref, amps_ref = refs[0], refs[1]
        pos = 2
        field_refs = refs[pos : pos + len(fields)]
        pos += len(fields)
        vel_ref, ani_ref = refs[pos : pos + 2]
        pos += 2
        left_refs = refs[pos : pos + n_side]
        pos += n_side
        right_refs = refs[pos : pos + n_side]
        pos += n_side
        other_hbm = refs[pos : pos + len(others)]
        pos += len(others)
        n_out = blocks if kind == "blocks" else 1
        outs = refs[pos : pos + n_out]
        pos += n_out
        buf_a, buf_b, v_buf, h_buf, c_buf, stage_l, stage_r, stage_t, top, beside, sums, sem = refs[
            pos : pos + 12
        ]

        steps = [ints_ref[k] for k in range(n_snaps)]
        first_row, skip, inside, source_x, source_y, place = [
            ints_ref[n_snaps + k] for k in range(6)
        ]
        window = pl.ds(pl.multiple_of(first_row, 8), rows)
        inner = pl.ds(PAD, rows)

        tile_copies = [
            pltpu.make_async_copy(
                vel_ref.at[:, window], v_buf.at[pl.ds(reach, width)], sem.at[0]
            ),
            pltpu.make_async_copy(
                ani_ref.at[:, window], h_buf.at[pl.ds(reach, width)], sem.at[1]
            ),
        ]
        side_copies = []
        where = 0
        offsets = []
        for depth, (pack, layer) in zip(depths, halo_at):
            n = len(side_copies)
            side_copies.append(
                pltpu.make_async_copy(
                    left_refs[pack].at[pl.ds(layer, depth)],
                    stage_l.at[pl.ds(where, depth)],
                    sem.at[2 + n],
                )
            )
            side_copies.append(
                pltpu.make_async_copy(
                    right_refs[pack].at[pl.ds(layer, depth)],
                    stage_r.at[pl.ds(where, depth)],
                    sem.at[3 + n],
                )
            )
            offsets.append(where)
            where += depth
        if packed:
            field_copies = [pltpu.make_async_copy(field_refs[0], stage_t, sem.at[12])]
        else:
            field_copies = [
                pltpu.make_async_copy(
                    field_refs[0].at[:, window], buf_a.at[pl.ds(reach, width), inner], sem.at[12]
                ),
                pltpu.make_async_copy(
                    field_refs[1].at[:, window], buf_b.at[pl.ds(reach, width), inner], sem.at[13]
                ),
            ]
            if backward:
                n_data = data.shape[0]
                flat = refs[-2]
                field_copies.append(
                    pltpu.make_async_copy(field_refs[2], flat.at[pl.ds(0, n_data)], sem.at[14])
                )
                flat[n_data:, :] = jnp.zeros((LANES - n_data, all_rows), jnp.float32)
        other_refs = refs[pos + 12 : pos + 12 + len(others)]
        other_copies = [
            pltpu.make_async_copy(source, target, sem.at[15 + n])
            for n, (source, target) in enumerate(zip(other_hbm, other_refs))
        ]
        for copy in tile_copies + side_copies + field_copies + other_copies:
            copy.start()
        beside[...] = neighbour_matrix()
        zeros = jnp.zeros((layers, PAD, LANES), jnp.float32)
        for buf in (buf_a, buf_b):
            buf[:, 0:PAD, :] = zeros
            buf[:, PAD + rows : PAD + rows + PAD, :] = zeros
        for copy in side_copies:
            copy.wait()

        def widen(stage, at, dst, first, count, row0, scale):
            def body(x, carry):
                for r0, size in spans(rows, 64):
                    code = stage[at + x, pl.ds(r0, size), :].astype(jnp.int32)
                    dst[first + x, pl.ds(row0 + r0, size), :] = code.astype(jnp.float32) * scale
                return carry

            lax.fori_loop(0, count, body, 0)

        side_scales = []
        for stage, starts in ((stage_l, (0, 1, 1, 1)), (stage_r, (reach + width,) * 4)):
            scale = decode_scale(stage, offsets[0], first_row, half_rows)
            side_scales.append(scale)
            for dst, at, start, depth, row0, unit in zip(
                (buf_a, buf_b, v_buf, h_buf), offsets, starts, depths, (PAD, PAD, 0, 0),
                (scale, scale, 1.0 / FIXED, 1.0 / FIXED),
            ):
                widen(stage, at, dst, start, depth, row0, unit)
        for copy in tile_copies:
            copy.wait()

        def coefficients(x, carry):
            for r0, size in spans(rows, 64):
                at = pl.ds(r0, size)
                v = v_buf[x, at, :]
                h = v * (1.0 + 2.0 * h_buf[x, at, :])
                h_buf[x, at, :] = h
                c_buf[x, at, :] = 2.0 - (4.0 * h + 2.0 * v)
            return carry

        lax.fori_loop(1, layers - 1, coefficients, 0)
        for copy in field_copies:
            copy.wait()
        if packed:
            scale = decode_scale(stage_t, field_at[0], first_row, half_rows)
            widen(stage_t, field_at[0], buf_a, reach, width, PAD, scale)
            widen(stage_t, field_at[1], buf_b, reach, width, PAD, scale)
        surface = None
        if backward:
            widen(stage_l, offsets[4], top, 0, 1, 0, side_scales[0])
            if packed:
                widen(stage_t, field_at[2], top, 1, 1, 0, scale)
            else:
                turned = refs[-1]
                turned[...] = flat[...].T
                top[1] = turned[window, :]
            widen(stage_r, offsets[4], top, 2, 1, 0, side_scales[1])

        if kind in ("image", "blocks"):
            image = outs[0] if kind == "image" else refs[-1]
            image[...] = jnp.zeros_like(image)

        def record(buf, time):
            slot, found = slot_of(steps, time)
            if kind in ("image", "blocks"):
                found = found & (inside > 0)

            @pl.when(found)
            def _():
                def body(x, carry):
                    for r0, size in spans(half_rows, 64):
                        base = pl.multiple_of(PAD + skip + r0, 8)
                        at = pl.ds(r0, size)
                        value = buf[reach + x, pl.ds(base, size), :]
                        if kind in ("snaps", "waves"):
                            outs[0][slot, x, at, :] = value.astype(outs[0].dtype)
                        elif kind == "image":
                            u = other_refs[0][slot, x, at, :].astype(jnp.float32)
                            image[x, at, :] = image[x, at, :] + u * value
                        else:
                            u = value.astype(jnp.bfloat16).astype(jnp.float32)
                            image[x, at, :] = image[x, at, :] + u * other_refs[1][slot, x, at, :]
                    return carry

                lax.fori_loop(0, width, body, 0)

        src, dst = buf_a, buf_b
        coefs = (c_buf, h_buf, v_buf)
        for copy in other_copies:
            copy.wait()
        record(src, reach + 1 if backward else 1)
        for step in range(1, reach + 1):
            lo, hi = step, layers - step
            if backward:

                def shift(x, step=step):
                    past = x - reach + width
                    plane = past // width
                    lane = (reach - step) * width + past - plane * width
                    return plane, lax.rem(LANES - lane, LANES)

                surface = (top, shift)
            stencil_step(src, dst, coefs, lo, hi, rows, beside, sums, surface)
            if not backward:
                row8 = lax.broadcasted_iota(jnp.int32, (8, LANES), 0)
                lane8 = lax.broadcasted_iota(jnp.int32, (8, LANES), 1)

                @pl.when((source_x >= lo) & (source_x < hi) & (source_y >= 0) & (source_y < rows))
                def _(dst=dst, step=step):
                    base = pl.multiple_of((source_y // 8) * 8, 8)
                    at = pl.ds(pl.multiple_of(base + PAD, 8), 8)
                    mask = (row8 == source_y - base) & (lane8 == 0)
                    add = v_buf[source_x, pl.ds(base, 8), :] * amps_ref[step - 1]
                    dst[source_x, at, :] = dst[source_x, at, :] + jnp.where(mask, add, 0.0)

            src, dst = dst, src
            record(src, reach + 1 - step if backward else step + 1)

        if kind == "blocks":
            block = half_rows // blocks
            for d, out in enumerate(outs):
                base = pl.multiple_of(lax.rem(place + d, blocks) * block, 8)

                def cut(x, carry, out=out, base=base):
                    at = pl.ds(base, block)
                    out[x] = other_refs[0][x, at, :] + image[x, at, :]
                    return carry

                lax.fori_loop(0, width, cut, 0)

    any_spec = pl.BlockSpec(memory_space=pl.ANY)
    smem = pl.BlockSpec(memory_space=pltpu.SMEM)
    vmem = pl.BlockSpec(memory_space=pltpu.VMEM)
    shape = (width, half_rows, depth_cells)
    if kind == "blocks":
        out_shape = (jax.ShapeDtypeStruct((width, half_rows // blocks, depth_cells), jnp.float32),) * blocks
    elif kind == "image":
        out_shape = (jax.ShapeDtypeStruct(shape, jnp.float32),)
    else:
        dtype = jnp.bfloat16 if kind == "snaps" else jnp.float32
        out_shape = (jax.ShapeDtypeStruct((n_snaps,) + shape, dtype),)
    cells = layers * rows * depth_cells
    grid_buf = pltpu.VMEM((layers, rows, depth_cells), jnp.float32)
    field_buf = pltpu.VMEM((layers, rows + 2 * PAD, depth_cells), jnp.float32)
    stage_layers = field.shape[0] if packed else 1
    side = pltpu.VMEM((sum(depths), rows, depth_cells), WIRE)
    return pl.pallas_call(
        kernel,
        out_shape=out_shape,
        in_specs=[smem, smem] + [any_spec] * (len(fields) + 2 + 2 * n_side + len(others)),
        out_specs=(vmem,) * len(out_shape),
        scratch_shapes=[
            field_buf, field_buf, grid_buf, grid_buf, grid_buf, side, side,
            pltpu.VMEM((stage_layers, rows, depth_cells), WIRE),
            pltpu.VMEM((3, rows, depth_cells), jnp.float32),
            pltpu.VMEM((2 * LANES, LANES), jnp.bfloat16),
            pltpu.VMEM((2, rows, depth_cells), jnp.float32),
            pltpu.SemaphoreType.DMA((18,)),
        ]
        + [pltpu.VMEM(other.shape, other.dtype) for other in others]
        + ([pltpu.VMEM(shape, jnp.float32)] if kind == "blocks" else [])
        + (
            [pltpu.VMEM((LANES, all_rows), jnp.float32), pltpu.VMEM((all_rows, LANES), jnp.float32)]
            if kind == "waves"
            else []
        ),
        cost_estimate=pl.CostEstimate(
            flops=15 * cells * reach, bytes_accessed=20 * cells, transcendentals=0
        ),
    )(ints, amps, *fields, vel, ani, *left, *right, *others)


def any_specs(n):
    return [pl.BlockSpec(memory_space=pl.ANY)] * n


def pack_rows(first, fields, ranges, groups, data):
    width, all_rows, depth_cells = fields[0].shape
    half_rows = all_rows // 2
    rows = half_rows + EDGE
    tail = 0 if data is None else 1
    sizes = [sum(hi - lo for _, lo, hi in r) + tail for r in ranges]
    n = len(fields)
    loose = [i for i in range(n) if not any(i in group for group in groups)]

    def kernel(first_ref, *refs):
        field_refs = refs[:n]
        outs = refs[n + tail : n + tail + len(ranges)]
        rest = refs[n + tail + len(ranges) :]
        wide, narrow, sem, out_sem = rest[:4]
        window = pl.ds(pl.multiple_of(first_ref[0], 16), rows)
        spare = pl.ds(pl.multiple_of(header_rows(first_ref[0], half_rows), 8), 8)
        copies = [
            pltpu.make_async_copy(ref.at[:, window], wide.at[i], sem.at[i])
            for i, ref in enumerate(field_refs)
        ]
        for copy in copies:
            copy.start()
        started = []

        def go(source, target):
            copy = pltpu.make_async_copy(source, target, out_sem.at[len(started)])
            copy.start()
            started.append(copy)

        def code(values, scale):
            return jnp.floor(values * scale + 0.5).astype(jnp.int32).astype(WIRE)

        def put(i, scale):
            def body(x, carry):
                for r0, size in spans(rows, 64):
                    at = pl.ds(r0, size)
                    narrow[i, x, at, :] = code(wide[i, x, at, :], scale)
                return carry

            lax.fori_loop(0, width, body, 0)
            for out, pieces in zip(outs, ranges):
                where = 0
                for field, lo, hi in pieces:
                    if field == i:
                        go(narrow.at[i, pl.ds(lo, hi - lo)], out.at[pl.ds(where, hi - lo)])
                    where += hi - lo

        for number, group in enumerate(groups):
            with_data = tail and number == len(groups) - 1
            if with_data:
                flat, turned = rest[4:6]
                load = pltpu.make_async_copy(refs[n], flat.at[pl.ds(0, data.shape[0])], sem.at[n])
                load.start()
                load.wait()
                flat[data.shape[0] :, :] = jnp.zeros((LANES - data.shape[0], all_rows), jnp.float32)
                turned[...] = flat[...].T
            top = jnp.zeros((8, LANES), jnp.float32)
            for i in group:
                copies[i].wait()

                def largest(x, top, i=i):
                    for r0, size in spans(rows, 64):
                        block = jnp.abs(wide[i, x, pl.ds(r0, size), :])
                        top = jnp.maximum(top, jnp.max(block.reshape(-1, 8, LANES), axis=0))
                    return top

                top = lax.fori_loop(0, width, largest, top)
            if with_data:
                block = jnp.abs(turned[window, :])
                top = jnp.maximum(top, jnp.max(block.reshape(-1, 8, LANES), axis=0))
            top = jnp.max(top, axis=(0, 1), keepdims=True)
            scale, unit, exponent = encode_scale(top)
            header = jnp.broadcast_to(exponent * unit, (8, LANES))
            for x in range(width):
                wide[group[0], x, spare, :] = header
            for i in group:
                put(i, scale)
            if with_data:
                narrow[n, 0] = code(turned[window, :], scale)
                for out, size in zip(outs, sizes):
                    go(narrow.at[n, pl.ds(0, 1)], out.at[pl.ds(size - 1, 1)])
        for i in loose:
            copies[i].wait()
            put(i, FIXED)
        for copy in started:
            copy.wait()

    n_out = sum(len(r) for r in ranges) + tail * len(ranges)
    scratch = [
        pltpu.VMEM((n, width, rows, depth_cells), jnp.float32),
        pltpu.VMEM((n + tail, width, rows, depth_cells), WIRE),
        pltpu.SemaphoreType.DMA((n + 1,)),
        pltpu.SemaphoreType.DMA((n_out,)),
    ]
    if tail:
        scratch += [
            pltpu.VMEM((LANES, all_rows), jnp.float32),
            pltpu.VMEM((all_rows, LANES), jnp.float32),
        ]
    cells = n * width * rows * depth_cells
    return pl.pallas_call(
        kernel,
        out_shape=tuple(jax.ShapeDtypeStruct((m, rows, depth_cells), WIRE) for m in sizes),
        in_specs=[pl.BlockSpec(memory_space=pltpu.SMEM)] + any_specs(n + tail),
        out_specs=tuple(any_specs(len(sizes))),
        scratch_shapes=scratch,
        cost_estimate=pl.CostEstimate(flops=cells, bytes_accessed=8 * cells, transcendentals=0),
        name="pack_rows",
    )(first, *fields, *([] if data is None else [data]))


def repack(packed, ranges):
    sizes = [sum(hi - lo for lo, hi in r) for r in ranges]
    n_out = sum(len(r) for r in ranges)

    def kernel(packed_ref, *refs):
        outs = refs[: len(ranges)]
        stage, sem, out_sem = refs[len(ranges) :]
        load = pltpu.make_async_copy(packed_ref, stage, sem.at[0])
        load.start()
        load.wait()
        started = []
        for out, pieces in zip(outs, ranges):
            where = 0
            for lo, hi in pieces:
                copy = pltpu.make_async_copy(
                    stage.at[pl.ds(lo, hi - lo)],
                    out.at[pl.ds(where, hi - lo)],
                    out_sem.at[len(started)],
                )
                copy.start()
                started.append(copy)
                where += hi - lo
        for copy in started:
            copy.wait()

    return pl.pallas_call(
        kernel,
        out_shape=tuple(jax.ShapeDtypeStruct((m,) + packed.shape[1:], packed.dtype) for m in sizes),
        in_specs=any_specs(1),
        out_specs=tuple(any_specs(len(sizes))),
        scratch_shapes=[
            pltpu.VMEM(packed.shape, packed.dtype),
            pltpu.SemaphoreType.DMA((1,)),
            pltpu.SemaphoreType.DMA((n_out,)),
        ],
        cost_estimate=pl.CostEstimate(
            flops=0, bytes_accessed=6 * packed.size, transcendentals=0
        ),
        name="repack",
    )(packed)


def on_device(
    fwd_prev,
    fwd_cur,
    bwd_next,
    bwd_cur,
    receiver_data,
    velocity_term,
    anisotropy,
    wavelet,
    shot_x,
    shot_y,
    aperture,
    snap_steps,
):
    shots = lax.axis_size("shot")
    tiles = lax.axis_size("xy")
    me = lax.axis_index("shot")
    tile = lax.axis_index("xy")
    half = shots // 2
    side = me // half
    partner = (me + half) % shots
    width, rows = fwd_prev.shape[1], fwd_prev.shape[2]
    reach = wavelet.shape[1]
    near = reach - 1
    n_snaps = snap_steps.shape[0]
    half_rows = rows // 2
    my_first = side * (half_rows - EDGE)
    their_first = (1 - side) * (half_rows - EDGE)
    across = [(i, (i + half) % shots) for i in range(shots)]
    up = [(i, i + 1) for i in range(tiles - 1)]
    down = [(i + 1, i) for i in range(tiles - 1)]
    u0, u1, w9, w8 = fwd_prev[0], fwd_cur[0], bwd_next[0], bwd_cur[0]

    data = receiver_data[0].reshape(reach * width, rows)

    def at(first):
        return jnp.reshape(first, (1,)).astype(jnp.int32)

    whole = ((0, 0, width), (1, 0, width))
    (send_w,) = pack_rows(at(their_first), (w8, w9), (whole,), ((0, 1),), data)
    import_w = lax.ppermute(send_w, "shot", across)

    def sides(fields, depths, groups, data):
        send_up, send_down = pack_rows(
            at(my_first), fields,
            (
                [(i, width - d, width) for i, d in enumerate(depths)],
                [(i, 0, d) for i, d in enumerate(depths)],
            ),
            groups, data,
        )
        from_left = lax.ppermute(send_up, "xy", up)
        from_right = lax.ppermute(send_down, "xy", down)
        return from_left, from_right

    left, right = sides(
        (u1, u0, velocity_term, anisotropy), (reach, near, near, near), ((0, 1),), None
    )
    left_l, right_l = sides((w8, w9), (reach, near), ((0, 1),), data)
    (send_u,) = pack_rows(at(their_first), (u1, u0), (whole,), ((0, 1),), None)
    import_u = lax.ppermute(send_u, "shot", across)

    def numbers(shot):
        chosen = (jnp.arange(shots, dtype=jnp.int32) == shot).astype(jnp.int32)
        source_x = jnp.sum(chosen * shot_x) - tile * width + reach
        source_y = jnp.sum(chosen * shot_y) - my_first
        inside = jnp.any((chosen[:, None] > 0) & (aperture == tile)).astype(jnp.int32)
        amps = jnp.sum(jnp.where(chosen[:, None] > 0, wavelet, 0.0), axis=0)
        parts = jnp.stack([my_first, side * EDGE, inside, source_x, source_y, me % half])
        return jnp.concatenate([snap_steps, parts]).astype(jnp.int32), amps

    ints_me, amps_me = numbers(me)
    ints_partner, amps_partner = numbers(partner)
    common = dict(half_rows=half_rows, reach=reach, n_snaps=n_snaps)
    at_v, at_a = (0, reach + near), (0, reach + 2 * near)
    (snaps,) = wave_pass(
        "snaps", (u1, u0), None, velocity_term, anisotropy, [left], [right],
        ((0, 0), (0, reach), at_v, at_a), ints_me, amps_me, **common,
    )

    def from_sides(packed, tail):
        ends = [(2 * width, 2 * width + 1)] if tail else []
        send_up, send_down = repack(
            packed,
            (
                [(width - reach, width), (2 * width - near, 2 * width)] + ends,
                [(0, reach), (width, width + near)] + ends,
            ),
        )
        from_left = lax.ppermute(send_up, "xy", up)
        from_right = lax.ppermute(send_down, "xy", down)
        return from_left, from_right

    (waves,) = wave_pass(
        "waves", (w8, w9), None, velocity_term, anisotropy, [left, left_l], [right, right_l],
        ((1, 0), (1, reach), at_v, at_a, (1, reach + near)),
        ints_partner, amps_partner, data=data, **common,
    )
    left_w, right_w = from_sides(import_w, True)
    (image,) = wave_pass(
        "image", import_w, (0, width, 2 * width), velocity_term, anisotropy,
        [left, left_w], [right, right_w],
        ((1, 0), (1, reach), at_v, at_a, (1, reach + near)),
        ints_me, amps_me, others=(snaps,), **common,
    )
    left_u, right_u = from_sides(import_u, False)
    blocks = wave_pass(
        "blocks", import_u, (0, width), velocity_term, anisotropy,
        [left, left_u], [right, right_u], ((1, 0), (1, reach), at_v, at_a),
        ints_partner, amps_partner, blocks=half, others=(image, waves), **common,
    )
    total = blocks[0]
    for d in range(1, half):
        route = [(i, (i // half) * half + (i % half + d) % half) for i in range(shots)]
        arrived = lax.ppermute(blocks[d], "shot", route)
        total = total + arrived
    return total


def solution(mesh):
    in_specs = (
        P("shot", "xy", None, None),
        P("shot", "xy", None, None),
        P("shot", "xy", None, None),
        P("shot", "xy", None, None),
        P("shot", None, "xy", None),
        P("xy", None, None),
        P("xy", None, None),
        P(),
        P(),
        P(),
        P(),
        P(),
    )
    out_specs = P("xy", "shot", None)

    return jax.shard_map(
        on_device, mesh=mesh, in_specs=in_specs, out_specs=out_specs, check_vma=False
    )
```

```python
import jax
import jax.numpy as jnp
from jax import lax
from jax.experimental import pallas as pl
from jax.experimental.pallas import tpu as pltpu
from jax.sharding import PartitionSpec as P


PAD = 8
EDGE = 16
LANES = 128
BY_MATRIX = ((True, False), (True, True))
CHUNK = 32
VMEM_OF_PASS = 67043328
WIRE = jnp.int16
STEPS_OF_SCALE = (32, 16, 8, 4, 2, 1)
FIXED = 65536.0


def spans(rows, chunk):
    return [(r0, min(chunk, rows - r0)) for r0 in range(0, rows, chunk)]


def neighbour_matrix():
    row = lax.broadcasted_iota(jnp.int32, (2 * LANES, LANES), 0)
    column = lax.broadcasted_iota(jnp.int32, (2 * LANES, LANES), 1)
    row = jnp.where(row >= LANES, row - LANES, row)
    beside = (row - column == 1) | (column - row == 1)
    return jnp.where(beside, 1.0, 0.0).astype(jnp.bfloat16)


def stencil_step(src, dst, coefs, lo, hi, rows, beside, sums, surface=None):
    centre, hor, vel = coefs
    by_matrix = BY_MATRIX[surface is not None]

    def vertical_sums(x, j):
        for r0, size in spans(rows, 144):
            c = src[x, pl.ds(PAD + r0, size), :]
            high = c.astype(jnp.bfloat16)
            low = (c - high.astype(jnp.float32)).astype(jnp.bfloat16)
            sums[j, pl.ds(r0, size), :] = jnp.dot(
                jnp.concatenate([high, low], axis=1), beside[...],
                preferred_element_type=jnp.float32,
            )

    def ahead(x):
        for j in range(2):
            if by_matrix[j]:
                vertical_sums(x + j, j)

    def body(i, carry):
        x = lo + 2 * i
        shifts = [None, None] if surface is None else [surface[1](x), surface[1](x + 1)]
        for r0, size in spans(rows, CHUNK):
            at = pl.ds(PAD + r0, size)
            here = pl.ds(r0, size)
            lane = lax.broadcasted_iota(jnp.int32, (size, LANES), 1)
            c = [src[x - 1 + j, at, :] for j in range(4)]
            for j in range(2):
                mid = c[j + 1]
                lateral = c[j] + c[j + 2]
                lateral = lateral + src[x + j, pl.ds(PAD + r0 - 1, size), :]
                lateral = lateral + src[x + j, pl.ds(PAD + r0 + 1, size), :]
                data = 0.0
                if surface is not None:
                    plane, shift = shifts[j]
                    data = pltpu.roll(surface[0][plane, here, :], shift, 1)
                if by_matrix[j]:
                    vertical = sums[j, here, :]
                    if surface is not None:
                        vertical = vertical + jnp.where(lane == 0, data, 0.0)
                else:
                    above = jnp.where(lane == 0, data, pltpu.roll(mid, 1, 1))
                    deeper = jnp.where(lane == LANES - 1, 0.0, pltpu.roll(mid, LANES - 1, 1))
                    vertical = above + deeper
                new = centre[x + j, here, :] * mid - dst[x + j, at, :]
                new = new + hor[x + j, here, :] * lateral
                new = new + vel[x + j, here, :] * vertical
                dst[x + j, at, :] = new
        ahead(jnp.minimum(x + 2, hi - 2))
        return carry

    ahead(lo)
    lax.fori_loop(0, (hi - lo) // 2, body, 0)


def header_rows(first, half_rows):
    return jnp.where(first == 0, half_rows + 8, 0)


def encode_scale(top):
    up, down, exponent = jnp.ones_like(top), jnp.ones_like(top), jnp.zeros_like(top)
    for j in STEPS_OF_SCALE:
        more = top * 2.0**j
        fits = more < 15.9
        top = jnp.where(fits, more, top)
        up = jnp.where(fits, up * 2.0**j, up)
        down = jnp.where(fits, down * 2.0**-j, down)
        exponent = jnp.where(fits, exponent + j, exponent)
    return up * 2048.0, down / 2048.0, exponent


def decode_scale(stage, layer, first, half_rows):
    base = pl.multiple_of(jnp.where(first == 0, half_rows, 0), 16)
    block = stage[layer, pl.ds(base, 16), :].astype(jnp.int32).astype(jnp.float32)
    row = lax.broadcasted_iota(jnp.int32, (16, LANES), 0)
    skip = jnp.where(first == 0, 8, 0)
    held = (row >= skip) & (row < skip + 8)
    exponent = jnp.max(jnp.where(held, block, 0.0), axis=(0, 1), keepdims=True)
    scale = jnp.full_like(exponent, 1.0 / 2048.0)
    for j in STEPS_OF_SCALE:
        holds = exponent >= j
        scale = jnp.where(holds, scale * 2.0**-j, scale)
        exponent = jnp.where(holds, exponent - j, exponent)
    return scale


def slot_of(steps, time):
    slot = jnp.int32(0)
    found = jnp.int32(0)
    for k, step in enumerate(steps):
        hit = (step == time).astype(jnp.int32)
        slot = slot + hit * k
        found = found + hit
    return slot, found > 0


def wave_pass(kind, field, field_at, vel, ani, left, right, halo_at, shot, ints, amps, half_rows, reach,
              n_snaps, blocks=1, others=(), data=None, model=None):
    width, all_rows, depth_cells = vel.shape
    rows = half_rows + EDGE
    layers = width + 2 * reach
    near = reach - 1
    backward = kind in ("waves", "image")
    packed = not isinstance(field, tuple)
    fields = [field] if packed else list(field) + ([data] if backward else [])
    first_pass = model is None
    depths = (reach, near) + ((near, near) if first_pass else ()) + ((1,) if backward else ())
    inputs_m = [vel, ani] if first_pass else list(model)
    n_side = len(left)

    def kernel(*refs):
        ints_ref, amps_ref = refs[0], refs[1]
        pos = 2
        field_refs = refs[pos : pos + len(fields)]
        pos += len(fields)
        model_refs = refs[pos : pos + len(inputs_m)]
        pos += len(inputs_m)
        left_refs = refs[pos : pos + n_side]
        pos += n_side
        right_refs = refs[pos : pos + n_side]
        pos += n_side
        other_hbm = refs[pos : pos + len(others)]
        pos += len(others)
        n_out = blocks if kind == "blocks" else 1
        n_model = 3 if first_pass else 0
        outs = refs[pos : pos + n_out]
        pos += n_out
        model_outs = refs[pos : pos + n_model]
        pos += n_model
        buf_a, buf_b, v_buf, h_buf, c_buf, stage_l, stage_r, stage_t, top, beside, sums, sem = refs[
            pos : pos + 12
        ]
        model_bufs = (c_buf, h_buf, v_buf)

        steps = [ints_ref[k] for k in range(n_snaps)]
        first_row, skip, place = [ints_ref[n_snaps + k] for k in range(3)]
        inside, source_x, source_y = [
            ints_ref[n_snaps + 3 + 2 * k + shot] for k in range(3)
        ]
        window = pl.ds(pl.multiple_of(first_row, 8), rows)
        inner = pl.ds(PAD, rows)

        tile_copies = []
        if first_pass:
            tile_copies = [
                pltpu.make_async_copy(
                    ref.at[:, window], buf.at[pl.ds(reach, width)], sem.at[n]
                )
                for n, (ref, buf) in enumerate(zip(model_refs, (v_buf, h_buf)))
            ]
        else:
            tile_copies = [
                pltpu.make_async_copy(ref, buf, sem.at[18 + n])
                for n, (ref, buf) in enumerate(zip(model_refs, model_bufs))
            ]
        side_copies = []
        where = 0
        offsets = []
        for depth, (pack, layer) in zip(depths, halo_at):
            n = len(side_copies)
            side_copies.append(
                pltpu.make_async_copy(
                    left_refs[pack].at[pl.ds(layer, depth)],
                    stage_l.at[pl.ds(where, depth)],
                    sem.at[2 + n],
                )
            )
            side_copies.append(
                pltpu.make_async_copy(
                    right_refs[pack].at[pl.ds(layer, depth)],
                    stage_r.at[pl.ds(where, depth)],
                    sem.at[3 + n],
                )
            )
            offsets.append(where)
            where += depth
        if packed:
            field_copies = [pltpu.make_async_copy(field_refs[0], stage_t, sem.at[12])]
        else:
            field_copies = [
                pltpu.make_async_copy(
                    field_refs[0].at[:, window], buf_a.at[pl.ds(reach, width), inner], sem.at[12]
                ),
                pltpu.make_async_copy(
                    field_refs[1].at[:, window], buf_b.at[pl.ds(reach, width), inner], sem.at[13]
                ),
            ]
            if backward:
                n_data = data.shape[0]
                flat = refs[-2]
                field_copies.append(
                    pltpu.make_async_copy(field_refs[2], flat.at[pl.ds(0, n_data)], sem.at[14])
                )
                flat[n_data:, :] = jnp.zeros((LANES - n_data, all_rows), jnp.float32)
        other_refs = refs[pos + 12 : pos + 12 + len(others)]
        other_copies = [
            pltpu.make_async_copy(source, target, sem.at[15 + n])
            for n, (source, target) in enumerate(zip(other_hbm, other_refs))
        ]
        in_order = tile_copies + side_copies + field_copies
        if not first_pass:
            in_order = side_copies + field_copies + tile_copies
        for copy in in_order + other_copies:
            copy.start()
        beside[...] = neighbour_matrix()
        zeros = jnp.zeros((layers, PAD, LANES), jnp.float32)
        for buf in (buf_a, buf_b):
            buf[:, 0:PAD, :] = zeros
            buf[:, PAD + rows : PAD + rows + PAD, :] = zeros
        for copy in side_copies:
            copy.wait()

        def widen(stage, at, dst, first, count, row0, scale):
            def body(x, carry):
                for r0, size in spans(rows, 64):
                    code = stage[at + x, pl.ds(r0, size), :].astype(jnp.int32)
                    dst[first + x, pl.ds(row0 + r0, size), :] = code.astype(jnp.float32) * scale
                return carry

            lax.fori_loop(0, count, body, 0)

        side_scales = []
        for stage, starts in ((stage_l, (0, 1, 1, 1)), (stage_r, (reach + width,) * 4)):
            scale = decode_scale(stage, offsets[0], first_row, half_rows)
            side_scales.append(scale)
            targets = (buf_a, buf_b) + ((v_buf, h_buf) if first_pass else ())
            for dst, at, start, depth, row0, unit in zip(
                targets, offsets, starts, depths, (PAD, PAD, 0, 0),
                (scale, scale, 1.0 / FIXED, 1.0 / FIXED),
            ):
                widen(stage, at, dst, start, depth, row0, unit)
        if first_pass:
            for copy in tile_copies:
                copy.wait()

        def coefficients(x, carry):
            for r0, size in spans(rows, 64):
                at = pl.ds(r0, size)
                v = v_buf[x, at, :]
                h = v * (1.0 + 2.0 * h_buf[x, at, :])
                h_buf[x, at, :] = h
                c_buf[x, at, :] = 2.0 - (4.0 * h + 2.0 * v)
            return carry

        model_copies = []
        if first_pass:
            edge = jnp.zeros((rows, LANES), jnp.float32)
            for buf in model_bufs:
                buf[0] = edge
                buf[layers - 1] = edge
            lax.fori_loop(1, layers - 1, coefficients, 0)
            model_copies = [
                pltpu.make_async_copy(buf, out, sem.at[18 + n])
                for n, (buf, out) in enumerate(zip(model_bufs, model_outs))
            ]
            for copy in model_copies:
                copy.start()
        for copy in field_copies:
            copy.wait()
        if packed:
            scale = decode_scale(stage_t, field_at[0], first_row, half_rows)
            widen(stage_t, field_at[0], buf_a, reach, width, PAD, scale)
            widen(stage_t, field_at[1], buf_b, reach, width, PAD, scale)
        surface = None
        if backward:
            widen(stage_l, offsets[-1], top, 0, 1, 0, side_scales[0])
            if packed:
                widen(stage_t, field_at[2], top, 1, 1, 0, scale)
            else:
                turned = refs[-1]
                turned[...] = flat[...].T
                top[1] = turned[window, :]
            widen(stage_r, offsets[-1], top, 2, 1, 0, side_scales[1])

        if kind in ("image", "blocks"):
            image = outs[0] if kind == "image" else refs[-1]
            image[...] = jnp.zeros_like(image)

        def record(buf, time):
            slot, found = slot_of(steps, time)
            if kind in ("image", "blocks"):
                found = found & (inside > 0)

            @pl.when(found)
            def _():
                def body(x, carry):
                    for r0, size in spans(half_rows, 64):
                        base = pl.multiple_of(PAD + skip + r0, 8)
                        at = pl.ds(r0, size)
                        value = buf[reach + x, pl.ds(base, size), :]
                        if kind in ("snaps", "waves"):
                            outs[0][slot, x, at, :] = value.astype(outs[0].dtype)
                        elif kind == "image":
                            u = other_refs[0][slot, x, at, :].astype(jnp.float32)
                            image[x, at, :] = image[x, at, :] + u * value
                        else:
                            u = value.astype(jnp.bfloat16).astype(jnp.float32)
                            image[x, at, :] = image[x, at, :] + u * other_refs[1][slot, x, at, :]
                    return carry

                lax.fori_loop(0, width, body, 0)

        src, dst = buf_a, buf_b
        coefs = (c_buf, h_buf, v_buf)
        if not first_pass:
            for copy in tile_copies:
                copy.wait()
        for copy in other_copies:
            copy.wait()
        record(src, reach + 1 if backward else 1)
        for step in range(1, reach + 1):
            lo, hi = step, layers - step
            if backward:

                def shift(x, step=step):
                    past = x - reach + width
                    plane = past // width
                    lane = (reach - step) * width + past - plane * width
                    return plane, lax.rem(LANES - lane, LANES)

                surface = (top, shift)
            stencil_step(src, dst, coefs, lo, hi, rows, beside, sums, surface)
            if not backward:
                row8 = lax.broadcasted_iota(jnp.int32, (8, LANES), 0)
                lane8 = lax.broadcasted_iota(jnp.int32, (8, LANES), 1)

                @pl.when((source_x >= lo) & (source_x < hi) & (source_y >= 0) & (source_y < rows))
                def _(dst=dst, step=step):
                    base = pl.multiple_of((source_y // 8) * 8, 8)
                    at = pl.ds(pl.multiple_of(base + PAD, 8), 8)
                    mask = (row8 == source_y - base) & (lane8 == 0)
                    add = v_buf[source_x, pl.ds(base, 8), :] * amps_ref[shot * reach + step - 1]
                    dst[source_x, at, :] = dst[source_x, at, :] + jnp.where(mask, add, 0.0)

            src, dst = dst, src
            record(src, reach + 1 - step if backward else step + 1)

        for copy in model_copies:
            copy.wait()
        if kind == "blocks":
            block = half_rows // blocks
            for d, out in enumerate(outs):
                base = pl.multiple_of(lax.rem(place + d, blocks) * block, 8)

                def cut(x, carry, out=out, base=base):
                    at = pl.ds(base, block)
                    out[x] = other_refs[0][x, at, :] + image[x, at, :]
                    return carry

                lax.fori_loop(0, width, cut, 0)

    any_spec = pl.BlockSpec(memory_space=pltpu.HBM)
    smem = pl.BlockSpec(memory_space=pltpu.SMEM)
    vmem = pl.BlockSpec(memory_space=pltpu.VMEM)
    shape = (width, half_rows, depth_cells)
    if kind == "blocks":
        out_shape = (jax.ShapeDtypeStruct((width, half_rows // blocks, depth_cells), jnp.float32),) * blocks
    elif kind == "image":
        out_shape = (jax.ShapeDtypeStruct(shape, jnp.float32),)
    else:
        dtype = jnp.bfloat16 if kind == "snaps" else jnp.float32
        out_shape = (jax.ShapeDtypeStruct((n_snaps,) + shape, dtype),)
    n_model = 3 if first_pass else 0
    if first_pass:
        out_shape += (jax.ShapeDtypeStruct((layers, rows, depth_cells), jnp.float32),) * 3
    cells = layers * rows * depth_cells
    grid_buf = pltpu.VMEM((layers, rows, depth_cells), jnp.float32)
    field_buf = pltpu.VMEM((layers, rows + 2 * PAD, depth_cells), jnp.float32)
    stage_layers = field.shape[0] if packed else 1
    side = pltpu.VMEM((sum(depths), rows, depth_cells), WIRE)
    return pl.pallas_call(
        kernel,
        out_shape=out_shape,
        in_specs=[smem, smem]
        + [any_spec] * len(fields)
        + [any_spec] * (len(inputs_m) + 2 * n_side + len(others)),
        out_specs=(vmem,) * (len(out_shape) - n_model) + (any_spec,) * n_model,
        scratch_shapes=[
            field_buf, field_buf, grid_buf, grid_buf, grid_buf, side, side,
            pltpu.VMEM((stage_layers, rows, depth_cells), WIRE),
            pltpu.VMEM((3, rows, depth_cells), jnp.float32),
            pltpu.VMEM((2 * LANES, LANES), jnp.bfloat16),
            pltpu.VMEM((2, rows, depth_cells), jnp.float32),
            pltpu.SemaphoreType.DMA((21,)),
        ]
        + [pltpu.VMEM(other.shape, other.dtype) for other in others]
        + ([pltpu.VMEM(shape, jnp.float32)] if kind == "blocks" else [])
        + (
            [pltpu.VMEM((LANES, all_rows), jnp.float32), pltpu.VMEM((all_rows, LANES), jnp.float32)]
            if kind == "waves"
            else []
        ),
        cost_estimate=pl.CostEstimate(
            flops=15 * cells * reach, bytes_accessed=20 * cells, transcendentals=0
        ),
        compiler_params=pltpu.CompilerParams(vmem_limit_bytes=VMEM_OF_PASS),
    )(ints, amps, *fields, *inputs_m, *left, *right, *others)


def any_specs(n):
    return [pl.BlockSpec(memory_space=pltpu.HBM)] * n


def pack_rows(first, fields, ranges, groups, data):
    width, all_rows, depth_cells = fields[0].shape
    half_rows = all_rows // 2
    rows = half_rows + EDGE
    tail = 0 if data is None else 1
    sizes = [sum(hi - lo for _, lo, hi in r) + tail for r in ranges]
    n = len(fields)
    loose = [i for i in range(n) if not any(i in group for group in groups)]

    def kernel(first_ref, *refs):
        field_refs = refs[:n]
        outs = refs[n + tail : n + tail + len(ranges)]
        rest = refs[n + tail + len(ranges) :]
        wide, narrow, sem, out_sem = rest[:4]
        window = pl.ds(pl.multiple_of(first_ref[0], 16), rows)
        spare = pl.ds(pl.multiple_of(header_rows(first_ref[0], half_rows), 8), 8)
        copies = [
            pltpu.make_async_copy(ref.at[:, window], wide.at[i], sem.at[i])
            for i, ref in enumerate(field_refs)
        ]
        for copy in copies:
            copy.start()
        started = []

        def go(source, target):
            copy = pltpu.make_async_copy(source, target, out_sem.at[len(started)])
            copy.start()
            started.append(copy)

        def code(values, scale):
            return jnp.floor(values * scale + 0.5).astype(jnp.int32).astype(WIRE)

        def put(i, scale):
            def body(x, carry):
                for r0, size in spans(rows, 64):
                    at = pl.ds(r0, size)
                    narrow[i, x, at, :] = code(wide[i, x, at, :], scale)
                return carry

            lax.fori_loop(0, width, body, 0)
            for out, pieces in zip(outs, ranges):
                where = 0
                for field, lo, hi in pieces:
                    if field == i:
                        go(narrow.at[i, pl.ds(lo, hi - lo)], out.at[pl.ds(where, hi - lo)])
                    where += hi - lo

        for number, group in enumerate(groups):
            with_data = tail and number == len(groups) - 1
            if with_data:
                flat, turned = rest[4:6]
                load = pltpu.make_async_copy(refs[n], flat.at[pl.ds(0, data.shape[0])], sem.at[n])
                load.start()
                load.wait()
                flat[data.shape[0] :, :] = jnp.zeros((LANES - data.shape[0], all_rows), jnp.float32)
                turned[...] = flat[...].T
            top = jnp.zeros((8, LANES), jnp.float32)
            for i in group:
                copies[i].wait()

                def largest(x, top, i=i):
                    for r0, size in spans(rows, 64):
                        block = jnp.abs(wide[i, x, pl.ds(r0, size), :])
                        top = jnp.maximum(top, jnp.max(block.reshape(-1, 8, LANES), axis=0))
                    return top

                top = lax.fori_loop(0, width, largest, top)
            if with_data:
                block = jnp.abs(turned[window, :])
                top = jnp.maximum(top, jnp.max(block.reshape(-1, 8, LANES), axis=0))
            top = jnp.max(top, axis=(0, 1), keepdims=True)
            scale, unit, exponent = encode_scale(top)
            header = jnp.broadcast_to(exponent * unit, (8, LANES))
            for x in range(width):
                wide[group[0], x, spare, :] = header
            for i in group:
                put(i, scale)
            if with_data:
                narrow[n, 0] = code(turned[window, :], scale)
                for out, size in zip(outs, sizes):
                    go(narrow.at[n, pl.ds(0, 1)], out.at[pl.ds(size - 1, 1)])
        for i in loose:
            copies[i].wait()
            put(i, FIXED)
        for copy in started:
            copy.wait()

    n_out = sum(len(r) for r in ranges) + tail * len(ranges)
    scratch = [
        pltpu.VMEM((n, width, rows, depth_cells), jnp.float32),
        pltpu.VMEM((n + tail, width, rows, depth_cells), WIRE),
        pltpu.SemaphoreType.DMA((n + 1,)),
        pltpu.SemaphoreType.DMA((n_out,)),
    ]
    if tail:
        scratch += [
            pltpu.VMEM((LANES, all_rows), jnp.float32),
            pltpu.VMEM((all_rows, LANES), jnp.float32),
        ]
    cells = n * width * rows * depth_cells
    return pl.pallas_call(
        kernel,
        out_shape=tuple(jax.ShapeDtypeStruct((m, rows, depth_cells), WIRE) for m in sizes),
        in_specs=[pl.BlockSpec(memory_space=pltpu.SMEM)] + any_specs(n + tail),
        out_specs=tuple(any_specs(len(sizes))),
        scratch_shapes=scratch,
        cost_estimate=pl.CostEstimate(flops=cells, bytes_accessed=8 * cells, transcendentals=0),
        name="pack_rows",
    )(first, *fields, *([] if data is None else [data]))


def repack(packed, ranges):
    sizes = [sum(hi - lo for lo, hi in r) for r in ranges]
    n_out = sum(len(r) for r in ranges)

    def kernel(packed_ref, *refs):
        outs = refs[: len(ranges)]
        stage, sem, out_sem = refs[len(ranges) :]
        load = pltpu.make_async_copy(packed_ref, stage, sem.at[0])
        load.start()
        load.wait()
        started = []
        for out, pieces in zip(outs, ranges):
            where = 0
            for lo, hi in pieces:
                copy = pltpu.make_async_copy(
                    stage.at[pl.ds(lo, hi - lo)],
                    out.at[pl.ds(where, hi - lo)],
                    out_sem.at[len(started)],
                )
                copy.start()
                started.append(copy)
                where += hi - lo
        for copy in started:
            copy.wait()

    return pl.pallas_call(
        kernel,
        out_shape=tuple(jax.ShapeDtypeStruct((m,) + packed.shape[1:], packed.dtype) for m in sizes),
        in_specs=any_specs(1),
        out_specs=tuple(any_specs(len(sizes))),
        scratch_shapes=[
            pltpu.VMEM(packed.shape, packed.dtype),
            pltpu.SemaphoreType.DMA((1,)),
            pltpu.SemaphoreType.DMA((n_out,)),
        ],
        cost_estimate=pl.CostEstimate(
            flops=0, bytes_accessed=6 * packed.size, transcendentals=0
        ),
        name="repack",
    )(packed)


def on_device(
    fwd_prev,
    fwd_cur,
    bwd_next,
    bwd_cur,
    receiver_data,
    velocity_term,
    anisotropy,
    wavelet,
    shot_x,
    shot_y,
    aperture,
    snap_steps,
):
    shots = lax.axis_size("shot")
    tiles = lax.axis_size("xy")
    me = lax.axis_index("shot")
    tile = lax.axis_index("xy")
    half = shots // 2
    side = me // half
    partner = (me + half) % shots
    width, rows = fwd_prev.shape[1], fwd_prev.shape[2]
    reach = wavelet.shape[1]
    near = reach - 1
    n_snaps = snap_steps.shape[0]
    half_rows = rows // 2
    my_first = side * (half_rows - EDGE)
    their_first = (1 - side) * (half_rows - EDGE)
    across = [(i, (i + half) % shots) for i in range(shots)]
    up = [(i, i + 1) for i in range(tiles - 1)]
    down = [(i + 1, i) for i in range(tiles - 1)]
    u0, u1, w9, w8 = fwd_prev[0], fwd_cur[0], bwd_next[0], bwd_cur[0]

    data = receiver_data[0].reshape(reach * width, rows)

    def at(first):
        return jnp.reshape(first, (1,)).astype(jnp.int32)

    whole = ((0, 0, width), (1, 0, width))
    (send_w,) = pack_rows(at(their_first), (w8, w9), (whole,), ((0, 1),), data)
    import_w = lax.ppermute(send_w, "shot", across)

    def sides(fields, depths, groups, data):
        send_up, send_down = pack_rows(
            at(my_first), fields,
            (
                [(i, width - d, width) for i, d in enumerate(depths)],
                [(i, 0, d) for i, d in enumerate(depths)],
            ),
            groups, data,
        )
        from_left = lax.ppermute(send_up, "xy", up)
        from_right = lax.ppermute(send_down, "xy", down)
        return from_left, from_right

    left, right = sides(
        (u1, u0, velocity_term, anisotropy), (reach, near, near, near), ((0, 1),), None
    )
    left_l, right_l = sides((w8, w9), (reach, near), ((0, 1),), data)
    (send_u,) = pack_rows(at(their_first), (u1, u0), (whole,), ((0, 1),), None)
    import_u = lax.ppermute(send_u, "shot", across)

    two = jnp.stack([me, partner])
    chosen = (jnp.arange(shots, dtype=jnp.int32)[None] == two[:, None]).astype(jnp.int32)
    source_x = jnp.sum(chosen * shot_x[None], axis=1) - tile * width + reach
    source_y = jnp.sum(chosen * shot_y[None], axis=1) - my_first
    here = jnp.any(aperture == tile, axis=1).astype(jnp.int32)
    inside = jnp.sum(chosen * here[None], axis=1)
    amps = jnp.sum(jnp.where(chosen[:, :, None] > 0, wavelet[None], 0.0), axis=1).reshape(-1)
    places = jnp.stack([my_first, side * EDGE, me % half])
    ints = jnp.concatenate([snap_steps, places, inside, source_x, source_y]).astype(jnp.int32)
    common = dict(half_rows=half_rows, reach=reach, n_snaps=n_snaps)
    at_v, at_a = (0, reach + near), (0, reach + 2 * near)
    snaps, *model = wave_pass(
        "snaps", (u1, u0), None, velocity_term, anisotropy, [left], [right],
        ((0, 0), (0, reach), at_v, at_a), 0, ints, amps, **common,
    )

    def from_sides(packed, tail):
        ends = [(2 * width, 2 * width + 1)] if tail else []
        send_up, send_down = repack(
            packed,
            (
                [(width - reach, width), (2 * width - near, 2 * width)] + ends,
                [(0, reach), (width, width + near)] + ends,
            ),
        )
        from_left = lax.ppermute(send_up, "xy", up)
        from_right = lax.ppermute(send_down, "xy", down)
        return from_left, from_right

    (waves,) = wave_pass(
        "waves", (w8, w9), None, velocity_term, anisotropy, [left_l], [right_l],
        ((0, 0), (0, reach), (0, reach + near)),
        1, ints, amps, data=data, model=model, **common,
    )
    left_w, right_w = from_sides(import_w, True)
    (image,) = wave_pass(
        "image", import_w, (0, width, 2 * width), velocity_term, anisotropy,
        [left_w], [right_w], ((0, 0), (0, reach), (0, reach + near)),
        0, ints, amps, others=(snaps,), model=model, **common,
    )
    left_u, right_u = from_sides(import_u, False)
    blocks = wave_pass(
        "blocks", import_u, (0, width), velocity_term, anisotropy,
        [left_u], [right_u], ((0, 0), (0, reach)),
        1, ints, amps, blocks=half, others=(image, waves), model=model, **common,
    )
    total = blocks[0]
    for d in range(1, half):
        route = [(i, (i // half) * half + (i % half + d) % half) for i in range(shots)]
        arrived = lax.ppermute(blocks[d], "shot", route)
        total = total + arrived
    return total


def solution(mesh):
    in_specs = (
        P("shot", "xy", None, None),
        P("shot", "xy", None, None),
        P("shot", "xy", None, None),
        P("shot", "xy", None, None),
        P("shot", None, "xy", None),
        P("xy", None, None),
        P("xy", None, None),
        P(),
        P(),
        P(),
        P(),
        P(),
    )
    out_specs = P("xy", "shot", None)

    return jax.shard_map(
        on_device, mesh=mesh, in_specs=in_specs, out_specs=out_specs, check_vma=False
    )
```

```python
import jax
import jax.numpy as jnp
from jax import lax
from jax.experimental import pallas as pl
from jax.experimental.pallas import tpu as pltpu
from jax.sharding import PartitionSpec as P


PAD = 8
EDGE = 16
LANES = 128
BY_MATRIX = ((True, False), (True, True))
CHUNK = 32
VMEM_OF_PASS = 67043328
WIRE = jnp.int16
STEPS_OF_SCALE = (32, 16, 8, 4, 2, 1)
FIXED = 65536.0


def spans(rows, chunk):
    return [(r0, min(chunk, rows - r0)) for r0 in range(0, rows, chunk)]


def neighbour_matrix():
    row = lax.broadcasted_iota(jnp.int32, (2 * LANES, LANES), 0)
    column = lax.broadcasted_iota(jnp.int32, (2 * LANES, LANES), 1)
    row = jnp.where(row >= LANES, row - LANES, row)
    beside = (row - column == 1) | (column - row == 1)
    return jnp.where(beside, 1.0, 0.0).astype(jnp.bfloat16)


def stencil_step(src, dst, coefs, lo, hi, rows, beside, sums, surface=None):
    centre, hor, vel = coefs
    by_matrix = BY_MATRIX[surface is not None]

    def vertical_sums(x, j):
        for r0, size in spans(rows, 144):
            c = src[x, pl.ds(PAD + r0, size), :]
            high = c.astype(jnp.bfloat16)
            low = (c - high.astype(jnp.float32)).astype(jnp.bfloat16)
            sums[j, pl.ds(r0, size), :] = jnp.dot(
                jnp.concatenate([high, low], axis=1), beside[...],
                preferred_element_type=jnp.float32,
            )

    def ahead(x):
        for j in range(2):
            if by_matrix[j]:
                vertical_sums(x + j, j)

    def body(i, carry):
        x = lo + 2 * i
        shifts = [None, None] if surface is None else [surface[1](x), surface[1](x + 1)]
        for r0, size in spans(rows, CHUNK):
            at = pl.ds(PAD + r0, size)
            here = pl.ds(r0, size)
            lane = lax.broadcasted_iota(jnp.int32, (size, LANES), 1)
            c = [src[x - 1 + j, at, :] for j in range(4)]
            for j in range(2):
                mid = c[j + 1]
                lateral = c[j] + c[j + 2]
                lateral = lateral + src[x + j, pl.ds(PAD + r0 - 1, size), :]
                lateral = lateral + src[x + j, pl.ds(PAD + r0 + 1, size), :]
                data = 0.0
                if surface is not None:
                    plane, shift = shifts[j]
                    data = pltpu.roll(surface[0][plane, here, :], shift, 1)
                if by_matrix[j]:
                    vertical = sums[j, here, :]
                    if surface is not None:
                        vertical = vertical + jnp.where(lane == 0, data, 0.0)
                else:
                    above = jnp.where(lane == 0, data, pltpu.roll(mid, 1, 1))
                    deeper = jnp.where(lane == LANES - 1, 0.0, pltpu.roll(mid, LANES - 1, 1))
                    vertical = above + deeper
                new = centre[x + j, here, :] * mid - dst[x + j, at, :]
                new = new + hor[x + j, here, :] * lateral
                new = new + vel[x + j, here, :] * vertical
                dst[x + j, at, :] = new
        ahead(jnp.minimum(x + 2, hi - 2))
        return carry

    ahead(lo)
    lax.fori_loop(0, (hi - lo) // 2, body, 0)


def header_rows(first, half_rows):
    return jnp.where(first == 0, half_rows + 8, 0)


def encode_scale(top):
    up, down, exponent = jnp.ones_like(top), jnp.ones_like(top), jnp.zeros_like(top)
    for j in STEPS_OF_SCALE:
        more = top * 2.0**j
        fits = more < 15.9
        top = jnp.where(fits, more, top)
        up = jnp.where(fits, up * 2.0**j, up)
        down = jnp.where(fits, down * 2.0**-j, down)
        exponent = jnp.where(fits, exponent + j, exponent)
    return up * 2048.0, down / 2048.0, exponent


def decode_scale(stage, layer, first, half_rows):
    base = pl.multiple_of(jnp.where(first == 0, half_rows, 0), 16)
    block = stage[layer, pl.ds(base, 16), :].astype(jnp.int32).astype(jnp.float32)
    row = lax.broadcasted_iota(jnp.int32, (16, LANES), 0)
    skip = jnp.where(first == 0, 8, 0)
    held = (row >= skip) & (row < skip + 8)
    exponent = jnp.max(jnp.where(held, block, 0.0), axis=(0, 1), keepdims=True)
    scale = jnp.full_like(exponent, 1.0 / 2048.0)
    for j in STEPS_OF_SCALE:
        holds = exponent >= j
        scale = jnp.where(holds, scale * 2.0**-j, scale)
        exponent = jnp.where(holds, exponent - j, exponent)
    return scale


def slot_of(steps, time):
    slot = jnp.int32(0)
    found = jnp.int32(0)
    for k, step in enumerate(steps):
        hit = (step == time).astype(jnp.int32)
        slot = slot + hit * k
        found = found + hit
    return slot, found > 0


def wave_pass(kind, field, field_at, vel, ani, left, right, halo_at, shot, ints, amps, half_rows, reach,
              n_snaps, blocks=1, others=(), data=None, model=None):
    width, all_rows, depth_cells = vel.shape
    rows = half_rows + EDGE
    layers = width + 2 * reach
    near = reach - 1
    backward = kind in ("waves", "image")
    packed = not isinstance(field, tuple)
    fields = [field] if packed else list(field) + ([data] if backward else [])
    first_pass = model is None
    depths = (reach, near) + ((near, near) if first_pass else ()) + ((1,) if backward else ())
    inputs_m = [vel, ani] if first_pass else list(model)
    n_side = len(left)

    def kernel(*refs):
        ints_ref, amps_ref = refs[0], refs[1]
        pos = 2
        field_refs = refs[pos : pos + len(fields)]
        pos += len(fields)
        model_refs = refs[pos : pos + len(inputs_m)]
        pos += len(inputs_m)
        left_refs = refs[pos : pos + n_side]
        pos += n_side
        right_refs = refs[pos : pos + n_side]
        pos += n_side
        other_hbm = refs[pos : pos + len(others)]
        pos += len(others)
        n_out = blocks if kind == "blocks" else 1
        n_model = 3 if first_pass else 0
        outs = refs[pos : pos + n_out]
        pos += n_out
        model_outs = refs[pos : pos + n_model]
        pos += n_model
        buf_a, buf_b, v_buf, h_buf, c_buf, stage_l, stage_r, stage_t, top, beside, sums, sem = refs[
            pos : pos + 12
        ]
        model_bufs = (c_buf, h_buf, v_buf)

        steps = [ints_ref[k] for k in range(n_snaps)]
        first_row, skip, place = [ints_ref[n_snaps + k] for k in range(3)]
        inside, source_x, source_y = [
            ints_ref[n_snaps + 3 + 2 * k + shot] for k in range(3)
        ]
        window = pl.ds(pl.multiple_of(first_row, 8), rows)
        inner = pl.ds(PAD, rows)

        tile_copies = []
        if first_pass:
            tile_copies = [
                pltpu.make_async_copy(
                    ref.at[:, window], buf.at[pl.ds(reach, width)], sem.at[n]
                )
                for n, (ref, buf) in enumerate(zip(model_refs, (v_buf, h_buf)))
            ]
        else:
            tile_copies = [
                pltpu.make_async_copy(ref, buf, sem.at[18 + n])
                for n, (ref, buf) in enumerate(zip(model_refs, model_bufs))
            ]
        side_copies = []
        where = 0
        offsets = []
        for depth, (pack, layer) in zip(depths, halo_at):
            n = len(side_copies)
            side_copies.append(
                pltpu.make_async_copy(
                    left_refs[pack].at[pl.ds(layer, depth)],
                    stage_l.at[pl.ds(where, depth)],
                    sem.at[2 + n],
                )
            )
            side_copies.append(
                pltpu.make_async_copy(
                    right_refs[pack].at[pl.ds(layer, depth)],
                    stage_r.at[pl.ds(where, depth)],
                    sem.at[3 + n],
                )
            )
            offsets.append(where)
            where += depth
        if packed:
            field_copies = [pltpu.make_async_copy(field_refs[0], stage_t, sem.at[12])]
        else:
            field_copies = [
                pltpu.make_async_copy(
                    field_refs[0].at[:, window], buf_a.at[pl.ds(reach, width), inner], sem.at[12]
                ),
                pltpu.make_async_copy(
                    field_refs[1].at[:, window], buf_b.at[pl.ds(reach, width), inner], sem.at[13]
                ),
            ]
            if backward:
                n_data = data.shape[0]
                flat = refs[-2]
                field_copies.append(
                    pltpu.make_async_copy(field_refs[2], flat.at[pl.ds(0, n_data)], sem.at[14])
                )
                flat[n_data:, :] = jnp.zeros((LANES - n_data, all_rows), jnp.float32)
        other_refs = refs[pos + 12 : pos + 12 + len(others)]
        other_copies = [
            pltpu.make_async_copy(source, target, sem.at[15 + n])
            for n, (source, target) in enumerate(zip(other_hbm, other_refs))
        ]
        in_order = tile_copies + side_copies + field_copies
        if not first_pass:
            in_order = side_copies + field_copies + tile_copies
        for copy in in_order + other_copies:
            copy.start()
        beside[...] = neighbour_matrix()
        zeros = jnp.zeros((layers, PAD, LANES), jnp.float32)
        for buf in (buf_a, buf_b):
            buf[:, 0:PAD, :] = zeros
            buf[:, PAD + rows : PAD + rows + PAD, :] = zeros
        for copy in side_copies:
            copy.wait()

        def widen(stage, at, dst, first, count, row0, scale):
            def body(x, carry):
                for r0, size in spans(rows, 64):
                    code = stage[at + x, pl.ds(r0, size), :].astype(jnp.int32)
                    dst[first + x, pl.ds(row0 + r0, size), :] = code.astype(jnp.float32) * scale
                return carry

            lax.fori_loop(0, count, body, 0)

        side_scales = []
        for stage, starts in ((stage_l, (0, 1, 1, 1)), (stage_r, (reach + width,) * 4)):
            scale = decode_scale(stage, offsets[0], first_row, half_rows)
            side_scales.append(scale)
            targets = (buf_a, buf_b) + ((v_buf, h_buf) if first_pass else ())
            for dst, at, start, depth, row0, unit in zip(
                targets, offsets, starts, depths, (PAD, PAD, 0, 0),
                (scale, scale, 1.0 / FIXED, 1.0 / FIXED),
            ):
                widen(stage, at, dst, start, depth, row0, unit)
        if first_pass:
            for copy in tile_copies:
                copy.wait()

        def coefficients(x, carry):
            for r0, size in spans(rows, 64):
                at = pl.ds(r0, size)
                v = v_buf[x, at, :]
                h = v * (1.0 + 2.0 * h_buf[x, at, :])
                h_buf[x, at, :] = h
                c_buf[x, at, :] = 2.0 - (4.0 * h + 2.0 * v)
            return carry

        model_copies = []
        if first_pass:
            edge = jnp.zeros((rows, LANES), jnp.float32)
            for buf in model_bufs:
                buf[0] = edge
                buf[layers - 1] = edge
            lax.fori_loop(1, layers - 1, coefficients, 0)
            model_copies = [
                pltpu.make_async_copy(buf, out, sem.at[18 + n])
                for n, (buf, out) in enumerate(zip(model_bufs, model_outs))
            ]
            for copy in model_copies:
                copy.start()
        for copy in field_copies:
            copy.wait()
        if packed:
            scale = decode_scale(stage_t, field_at[0], first_row, half_rows)
            widen(stage_t, field_at[0], buf_a, reach, width, PAD, scale)
            widen(stage_t, field_at[1], buf_b, reach, width, PAD, scale)
        surface = None
        if backward:
            widen(stage_l, offsets[-1], top, 0, 1, 0, side_scales[0])
            if packed:
                widen(stage_t, field_at[2], top, 1, 1, 0, scale)
            else:
                turned = refs[-1]
                turned[...] = flat[...].T
                top[1] = turned[window, :]
            widen(stage_r, offsets[-1], top, 2, 1, 0, side_scales[1])

        if kind in ("image", "blocks"):
            image = outs[0] if kind == "image" else refs[-1]
            image[...] = jnp.zeros_like(image)

        def record(buf, time):
            slot, found = slot_of(steps, time)
            if kind in ("image", "blocks"):
                found = found & (inside > 0)

            @pl.when(found)
            def _():
                def body(x, carry):
                    for r0, size in spans(half_rows, 64):
                        base = pl.multiple_of(PAD + skip + r0, 8)
                        at = pl.ds(r0, size)
                        value = buf[reach + x, pl.ds(base, size), :]
                        if kind in ("snaps", "waves"):
                            outs[0][slot, x, at, :] = value.astype(outs[0].dtype)
                        elif kind == "image":
                            u = other_refs[0][slot, x, at, :].astype(jnp.float32)
                            image[x, at, :] = image[x, at, :] + u * value
                        else:
                            u = value.astype(jnp.bfloat16).astype(jnp.float32)
                            image[x, at, :] = image[x, at, :] + u * other_refs[1][slot, x, at, :]
                    return carry

                lax.fori_loop(0, width, body, 0)

        src, dst = buf_a, buf_b
        coefs = (c_buf, h_buf, v_buf)
        if not first_pass:
            for copy in tile_copies:
                copy.wait()
        for step in range(1, reach + 1):
            lo, hi = step, layers - step
            if backward:

                def shift(x, step=step):
                    past = x - reach + width
                    plane = past // width
                    lane = (reach - step) * width + past - plane * width
                    return plane, lax.rem(LANES - lane, LANES)

                surface = (top, shift)
            stencil_step(src, dst, coefs, lo, hi, rows, beside, sums, surface)
            if not backward:
                row8 = lax.broadcasted_iota(jnp.int32, (8, LANES), 0)
                lane8 = lax.broadcasted_iota(jnp.int32, (8, LANES), 1)

                @pl.when((source_x >= lo) & (source_x < hi) & (source_y >= 0) & (source_y < rows))
                def _(dst=dst, step=step):
                    base = pl.multiple_of((source_y // 8) * 8, 8)
                    at = pl.ds(pl.multiple_of(base + PAD, 8), 8)
                    mask = (row8 == source_y - base) & (lane8 == 0)
                    add = v_buf[source_x, pl.ds(base, 8), :] * amps_ref[shot * reach + step - 1]
                    dst[source_x, at, :] = dst[source_x, at, :] + jnp.where(mask, add, 0.0)

            if step == 1:
                for copy in other_copies[-1:]:
                    copy.wait()
                record(src, reach + 1 if backward else 1)
            src, dst = dst, src
            record(src, reach + 1 - step if backward else step + 1)

        for copy in model_copies + other_copies[:-1]:
            copy.wait()
        if kind == "blocks":
            block = half_rows // blocks
            for d, out in enumerate(outs):
                base = pl.multiple_of(lax.rem(place + d, blocks) * block, 8)

                def cut(x, carry, out=out, base=base):
                    at = pl.ds(base, block)
                    out[x] = (other_refs[0][x, at, :] + image[x, at, :]).astype(out.dtype)
                    return carry

                lax.fori_loop(0, width, cut, 0)

    any_spec = pl.BlockSpec(memory_space=pltpu.HBM)
    smem = pl.BlockSpec(memory_space=pltpu.SMEM)
    vmem = pl.BlockSpec(memory_space=pltpu.VMEM)
    shape = (width, half_rows, depth_cells)
    if kind == "blocks":
        block_shape = (width, half_rows // blocks, depth_cells)
        out_shape = (jax.ShapeDtypeStruct(block_shape, jnp.float32),)
        out_shape += (jax.ShapeDtypeStruct(block_shape, jnp.bfloat16),) * (blocks - 1)
    elif kind == "image":
        out_shape = (jax.ShapeDtypeStruct(shape, jnp.float32),)
    else:
        dtype = jnp.bfloat16 if kind == "snaps" else jnp.float32
        out_shape = (jax.ShapeDtypeStruct((n_snaps,) + shape, dtype),)
    n_model = 3 if first_pass else 0
    if first_pass:
        out_shape += (jax.ShapeDtypeStruct((layers, rows, depth_cells), jnp.float32),) * 3
    cells = layers * rows * depth_cells
    grid_buf = pltpu.VMEM((layers, rows, depth_cells), jnp.float32)
    field_buf = pltpu.VMEM((layers, rows + 2 * PAD, depth_cells), jnp.float32)
    stage_layers = field.shape[0] if packed else 1
    side = pltpu.VMEM((sum(depths), rows, depth_cells), WIRE)
    return pl.pallas_call(
        kernel,
        out_shape=out_shape,
        in_specs=[smem, smem]
        + [any_spec] * len(fields)
        + [any_spec] * (len(inputs_m) + 2 * n_side + len(others)),
        out_specs=(vmem,) * (len(out_shape) - n_model) + (any_spec,) * n_model,
        scratch_shapes=[
            field_buf, field_buf, grid_buf, grid_buf, grid_buf, side, side,
            pltpu.VMEM((stage_layers, rows, depth_cells), WIRE),
            pltpu.VMEM((3, rows, depth_cells), jnp.float32),
            pltpu.VMEM((2 * LANES, LANES), jnp.bfloat16),
            pltpu.VMEM((2, rows, depth_cells), jnp.float32),
            pltpu.SemaphoreType.DMA((21,)),
        ]
        + [pltpu.VMEM(other.shape, other.dtype) for other in others]
        + ([pltpu.VMEM(shape, jnp.float32)] if kind == "blocks" else [])
        + (
            [pltpu.VMEM((LANES, all_rows), jnp.float32), pltpu.VMEM((all_rows, LANES), jnp.float32)]
            if kind == "waves"
            else []
        ),
        cost_estimate=pl.CostEstimate(
            flops=15 * cells * reach, bytes_accessed=20 * cells, transcendentals=0
        ),
        compiler_params=pltpu.CompilerParams(vmem_limit_bytes=VMEM_OF_PASS),
    )(ints, amps, *fields, *inputs_m, *left, *right, *others)


def any_specs(n):
    return [pl.BlockSpec(memory_space=pltpu.HBM)] * n


def pack_rows(first, fields, ranges, groups, data):
    width, all_rows, depth_cells = fields[0].shape
    half_rows = all_rows // 2
    rows = half_rows + EDGE
    tail = 0 if data is None else 1
    sizes = [sum(hi - lo for _, lo, hi in r) + tail for r in ranges]
    n = len(fields)
    loose = [i for i in range(n) if not any(i in group for group in groups)]

    def kernel(first_ref, *refs):
        field_refs = refs[:n]
        outs = refs[n + tail : n + tail + len(ranges)]
        rest = refs[n + tail + len(ranges) :]
        wide, narrow, sem, out_sem = rest[:4]
        window = pl.ds(pl.multiple_of(first_ref[0], 16), rows)
        spare = pl.ds(pl.multiple_of(header_rows(first_ref[0], half_rows), 8), 8)
        copies = [
            pltpu.make_async_copy(ref.at[:, window], wide.at[i], sem.at[i])
            for i, ref in enumerate(field_refs)
        ]
        for copy in copies:
            copy.start()
        started = []

        def go(source, target):
            copy = pltpu.make_async_copy(source, target, out_sem.at[len(started)])
            copy.start()
            started.append(copy)

        def code(values, scale):
            return jnp.floor(values * scale + 0.5).astype(jnp.int32).astype(WIRE)

        def put(i, scale):
            def body(x, carry):
                for r0, size in spans(rows, 64):
                    at = pl.ds(r0, size)
                    narrow[i, x, at, :] = code(wide[i, x, at, :], scale)
                return carry

            lax.fori_loop(0, width, body, 0)
            for out, pieces in zip(outs, ranges):
                where = 0
                for field, lo, hi in pieces:
                    if field == i:
                        go(narrow.at[i, pl.ds(lo, hi - lo)], out.at[pl.ds(where, hi - lo)])
                    where += hi - lo

        for number, group in enumerate(groups):
            with_data = tail and number == len(groups) - 1
            if with_data:
                flat, turned = rest[4:6]
                load = pltpu.make_async_copy(refs[n], flat.at[pl.ds(0, data.shape[0])], sem.at[n])
                load.start()
                load.wait()
                flat[data.shape[0] :, :] = jnp.zeros((LANES - data.shape[0], all_rows), jnp.float32)
                turned[...] = flat[...].T
            top = jnp.zeros((8, LANES), jnp.float32)
            for i in group:
                copies[i].wait()

                def largest(x, top, i=i):
                    for r0, size in spans(rows, 64):
                        block = jnp.abs(wide[i, x, pl.ds(r0, size), :])
                        top = jnp.maximum(top, jnp.max(block.reshape(-1, 8, LANES), axis=0))
                    return top

                top = lax.fori_loop(0, width, largest, top)
            if with_data:
                block = jnp.abs(turned[window, :])
                top = jnp.maximum(top, jnp.max(block.reshape(-1, 8, LANES), axis=0))
            top = jnp.max(top, axis=(0, 1), keepdims=True)
            scale, unit, exponent = encode_scale(top)
            header = jnp.broadcast_to(exponent * unit, (8, LANES))
            for x in range(width):
                wide[group[0], x, spare, :] = header
            for i in group:
                put(i, scale)
            if with_data:
                narrow[n, 0] = code(turned[window, :], scale)
                for out, size in zip(outs, sizes):
                    go(narrow.at[n, pl.ds(0, 1)], out.at[pl.ds(size - 1, 1)])
        for i in loose:
            copies[i].wait()
            put(i, FIXED)
        for copy in started:
            copy.wait()

    n_out = sum(len(r) for r in ranges) + tail * len(ranges)
    scratch = [
        pltpu.VMEM((n, width, rows, depth_cells), jnp.float32),
        pltpu.VMEM((n + tail, width, rows, depth_cells), WIRE),
        pltpu.SemaphoreType.DMA((n + 1,)),
        pltpu.SemaphoreType.DMA((n_out,)),
    ]
    if tail:
        scratch += [
            pltpu.VMEM((LANES, all_rows), jnp.float32),
            pltpu.VMEM((all_rows, LANES), jnp.float32),
        ]
    cells = n * width * rows * depth_cells
    return pl.pallas_call(
        kernel,
        out_shape=tuple(jax.ShapeDtypeStruct((m, rows, depth_cells), WIRE) for m in sizes),
        in_specs=[pl.BlockSpec(memory_space=pltpu.SMEM)] + any_specs(n + tail),
        out_specs=tuple(any_specs(len(sizes))),
        scratch_shapes=scratch,
        cost_estimate=pl.CostEstimate(flops=cells, bytes_accessed=8 * cells, transcendentals=0),
        name="pack_rows",
    )(first, *fields, *([] if data is None else [data]))


def repack(packed, ranges):
    sizes = [sum(hi - lo for lo, hi in r) for r in ranges]
    n_out = sum(len(r) for r in ranges)

    def kernel(packed_ref, *refs):
        outs = refs[: len(ranges)]
        stage, sem, out_sem = refs[len(ranges) :]
        load = pltpu.make_async_copy(packed_ref, stage, sem.at[0])
        load.start()
        load.wait()
        started = []
        for out, pieces in zip(outs, ranges):
            where = 0
            for lo, hi in pieces:
                copy = pltpu.make_async_copy(
                    stage.at[pl.ds(lo, hi - lo)],
                    out.at[pl.ds(where, hi - lo)],
                    out_sem.at[len(started)],
                )
                copy.start()
                started.append(copy)
                where += hi - lo
        for copy in started:
            copy.wait()

    return pl.pallas_call(
        kernel,
        out_shape=tuple(jax.ShapeDtypeStruct((m,) + packed.shape[1:], packed.dtype) for m in sizes),
        in_specs=any_specs(1),
        out_specs=tuple(any_specs(len(sizes))),
        scratch_shapes=[
            pltpu.VMEM(packed.shape, packed.dtype),
            pltpu.SemaphoreType.DMA((1,)),
            pltpu.SemaphoreType.DMA((n_out,)),
        ],
        cost_estimate=pl.CostEstimate(
            flops=0, bytes_accessed=6 * packed.size, transcendentals=0
        ),
        name="repack",
    )(packed)


def on_device(
    fwd_prev,
    fwd_cur,
    bwd_next,
    bwd_cur,
    receiver_data,
    velocity_term,
    anisotropy,
    wavelet,
    shot_x,
    shot_y,
    aperture,
    snap_steps,
):
    shots = lax.axis_size("shot")
    tiles = lax.axis_size("xy")
    me = lax.axis_index("shot")
    tile = lax.axis_index("xy")
    half = shots // 2
    side = me // half
    partner = (me + half) % shots
    width, rows = fwd_prev.shape[1], fwd_prev.shape[2]
    reach = wavelet.shape[1]
    near = reach - 1
    n_snaps = snap_steps.shape[0]
    half_rows = rows // 2
    my_first = side * (half_rows - EDGE)
    their_first = (1 - side) * (half_rows - EDGE)
    across = [(i, (i + half) % shots) for i in range(shots)]
    up = [(i, i + 1) for i in range(tiles - 1)]
    down = [(i + 1, i) for i in range(tiles - 1)]
    u0, u1, w9, w8 = fwd_prev[0], fwd_cur[0], bwd_next[0], bwd_cur[0]

    data = receiver_data[0].reshape(reach * width, rows)

    def at(first):
        return jnp.reshape(first, (1,)).astype(jnp.int32)

    whole = ((0, 0, width), (1, 0, width))
    (send_w,) = pack_rows(at(their_first), (w8, w9), (whole,), ((0, 1),), data)
    import_w = lax.ppermute(send_w, "shot", across)

    def sides(fields, depths, groups, data):
        send_up, send_down = pack_rows(
            at(my_first), fields,
            (
                [(i, width - d, width) for i, d in enumerate(depths)],
                [(i, 0, d) for i, d in enumerate(depths)],
            ),
            groups, data,
        )
        from_left = lax.ppermute(send_up, "xy", up)
        from_right = lax.ppermute(send_down, "xy", down)
        return from_left, from_right

    left, right = sides(
        (u1, u0, velocity_term, anisotropy), (reach, near, near, near), ((0, 1),), None
    )
    left_l, right_l = sides((w8, w9), (reach, near), ((0, 1),), data)
    (send_u,) = pack_rows(at(their_first), (u1, u0), (whole,), ((0, 1),), None)
    import_u = lax.ppermute(send_u, "shot", across)

    two = jnp.stack([me, partner])
    chosen = (jnp.arange(shots, dtype=jnp.int32)[None] == two[:, None]).astype(jnp.int32)
    source_x = jnp.sum(chosen * shot_x[None], axis=1) - tile * width + reach
    source_y = jnp.sum(chosen * shot_y[None], axis=1) - my_first
    here = jnp.any(aperture == tile, axis=1).astype(jnp.int32)
    inside = jnp.sum(chosen * here[None], axis=1)
    amps = jnp.sum(jnp.where(chosen[:, :, None] > 0, wavelet[None], 0.0), axis=1).reshape(-1)
    places = jnp.stack([my_first, side * EDGE, me % half])
    ints = jnp.concatenate([snap_steps, places, inside, source_x, source_y]).astype(jnp.int32)
    common = dict(half_rows=half_rows, reach=reach, n_snaps=n_snaps)
    at_v, at_a = (0, reach + near), (0, reach + 2 * near)
    snaps, *model = wave_pass(
        "snaps", (u1, u0), None, velocity_term, anisotropy, [left], [right],
        ((0, 0), (0, reach), at_v, at_a), 0, ints, amps, **common,
    )

    def from_sides(packed, tail):
        ends = [(2 * width, 2 * width + 1)] if tail else []
        send_up, send_down = repack(
            packed,
            (
                [(width - reach, width), (2 * width - near, 2 * width)] + ends,
                [(0, reach), (width, width + near)] + ends,
            ),
        )
        from_left = lax.ppermute(send_up, "xy", up)
        from_right = lax.ppermute(send_down, "xy", down)
        return from_left, from_right

    (waves,) = wave_pass(
        "waves", (w8, w9), None, velocity_term, anisotropy, [left_l], [right_l],
        ((0, 0), (0, reach), (0, reach + near)),
        1, ints, amps, data=data, model=model, **common,
    )
    left_w, right_w = from_sides(import_w, True)
    (image,) = wave_pass(
        "image", import_w, (0, width, 2 * width), velocity_term, anisotropy,
        [left_w], [right_w], ((0, 0), (0, reach), (0, reach + near)),
        0, ints, amps, others=(snaps,), model=model, **common,
    )
    left_u, right_u = from_sides(import_u, False)
    blocks = wave_pass(
        "blocks", import_u, (0, width), velocity_term, anisotropy,
        [left_u], [right_u], ((0, 0), (0, reach)),
        1, ints, amps, blocks=half, others=(image, waves), model=model, **common,
    )
    total = blocks[0]
    for d in range(1, half):
        route = [(i, (i // half) * half + (i % half + d) % half) for i in range(shots)]
        arrived = lax.ppermute(blocks[d], "shot", route)
        total = total + arrived.astype(jnp.float32)
    return total


def solution(mesh):
    in_specs = (
        P("shot", "xy", None, None),
        P("shot", "xy", None, None),
        P("shot", "xy", None, None),
        P("shot", "xy", None, None),
        P("shot", None, "xy", None),
        P("xy", None, None),
        P("xy", None, None),
        P(),
        P(),
        P(),
        P(),
        P(),
    )
    out_specs = P("xy", "shot", None)

    return jax.shard_map(
        on_device, mesh=mesh, in_specs=in_specs, out_specs=out_specs, check_vma=False
    )
```

```python
import jax
import jax.numpy as jnp
from jax import lax
from jax.experimental import pallas as pl
from jax.experimental.pallas import tpu as pltpu
from jax.sharding import PartitionSpec as P


PAD = 8
EDGE = 8
LANES = 128
BY_MATRIX = ((True, False), (True, True))
CHUNK = 32
VMEM_OF_PASS = 67043328
WIRE = jnp.int16
STEPS_OF_SCALE = (32, 16, 8, 4, 2, 1)
FIXED = 65536.0


def spans(rows, chunk):
    return [(r0, min(chunk, rows - r0)) for r0 in range(0, rows, chunk)]


def neighbour_matrix():
    row = lax.broadcasted_iota(jnp.int32, (2 * LANES, LANES), 0)
    column = lax.broadcasted_iota(jnp.int32, (2 * LANES, LANES), 1)
    row = jnp.where(row >= LANES, row - LANES, row)
    beside = (row - column == 1) | (column - row == 1)
    return jnp.where(beside, 1.0, jnp.where(row == column, -2.0, 0.0)).astype(jnp.bfloat16)


def stencil_step(src, dst, coefs, lo, hi, rows, beside, sums, surface=None):
    hor, vel = coefs
    by_matrix = BY_MATRIX[surface is not None]

    def vertical_sums(x, j):
        for r0, size in spans(rows, 144):
            c = src[x, pl.ds(PAD + r0, size), :]
            high = c.astype(jnp.bfloat16)
            low = (c - high.astype(jnp.float32)).astype(jnp.bfloat16)
            sums[j, pl.ds(r0, size), :] = jnp.dot(
                jnp.concatenate([high, low], axis=1), beside[...],
                preferred_element_type=jnp.float32,
            )

    def ahead(x):
        for j in range(2):
            if by_matrix[j]:
                vertical_sums(x + j, j)

    def body(i, carry):
        x = lo + 2 * i
        if surface is None:
            ahead(x)
        shifts = [None, None] if surface is None else [surface[1](x), surface[1](x + 1)]
        for r0, size in spans(rows, CHUNK):
            at = pl.ds(PAD + r0, size)
            here = pl.ds(r0, size)
            lane = lax.broadcasted_iota(jnp.int32, (size, LANES), 1)
            c = [src[x - 1 + j, at, :] for j in range(4)]
            for j in range(2):
                mid = c[j + 1]
                lateral = c[j] + c[j + 2]
                lateral = lateral + src[x + j, pl.ds(PAD + r0 - 1, size), :]
                lateral = lateral + src[x + j, pl.ds(PAD + r0 + 1, size), :]
                data = 0.0
                if surface is not None:
                    plane, shift = shifts[j]
                    data = pltpu.roll(surface[0][plane, here, :], shift, 1)
                if by_matrix[j]:
                    vertical = sums[j, here, :]
                    if surface is not None:
                        vertical = vertical + jnp.where(lane == 0, data, 0.0)
                else:
                    above = jnp.where(lane == 0, data, pltpu.roll(mid, 1, 1))
                    deeper = jnp.where(lane == LANES - 1, 0.0, pltpu.roll(mid, LANES - 1, 1))
                    vertical = above + deeper - (mid + mid)
                twice = mid + mid
                new = twice - dst[x + j, at, :]
                new = new + hor[x + j, here, :] * (lateral - (twice + twice))
                new = new + vel[x + j, here, :] * vertical
                dst[x + j, at, :] = new
        if surface is not None:
            ahead(jnp.minimum(x + 2, hi - 2))
        return carry

    if surface is not None:
        ahead(lo)
    lax.fori_loop(0, (hi - lo) // 2, body, 0)


def spare_row(first, half_rows):
    return pl.multiple_of(jnp.where(first == 0, half_rows, 0), 8), jnp.where(first == 0, 7, 0)


def encode_scale(top):
    up, down, exponent = jnp.ones_like(top), jnp.ones_like(top), jnp.zeros_like(top)
    for j in STEPS_OF_SCALE:
        more = top * 2.0**j
        fits = more < 15.9
        top = jnp.where(fits, more, top)
        up = jnp.where(fits, up * 2.0**j, up)
        down = jnp.where(fits, down * 2.0**-j, down)
        exponent = jnp.where(fits, exponent + j, exponent)
    return up * 2048.0, down / 2048.0, exponent


def decode_scale(stage, layer, first, half_rows):
    base, spare = spare_row(first, half_rows)
    block = stage[layer, pl.ds(base, 8), :].astype(jnp.int32).astype(jnp.float32)
    held = lax.broadcasted_iota(jnp.int32, (8, LANES), 0) == spare
    exponent = jnp.max(jnp.where(held, block, 0.0), axis=(0, 1), keepdims=True)
    scale = jnp.full_like(exponent, 1.0 / 2048.0)
    for j in STEPS_OF_SCALE:
        holds = exponent >= j
        scale = jnp.where(holds, scale * 2.0**-j, scale)
        exponent = jnp.where(holds, exponent - j, exponent)
    return scale


def slot_of(steps, time):
    slot = jnp.int32(0)
    found = jnp.int32(0)
    for k, step in enumerate(steps):
        hit = (step == time).astype(jnp.int32)
        slot = slot + hit * k
        found = found + hit
    return slot, found > 0


def wave_pass(kind, field, field_at, vel, ani, left, right, halo_at, shot, ints, amps, half_rows, reach,
              n_snaps, blocks=1, others=(), data=None, model=None):
    width, all_rows, depth_cells = vel.shape
    rows = half_rows + EDGE
    layers = width + 2 * reach
    near = reach - 1
    backward = kind in ("waves", "image")
    packed = not isinstance(field, tuple)
    fields = [field] if packed else list(field) + ([data] if backward else [])
    first_pass = model is None
    depths = (reach, near) + ((near, near) if first_pass else ()) + ((1,) if backward else ())
    inputs_m = [vel, ani] if first_pass else list(model)
    n_side = len(left)

    def kernel(*refs):
        ints_ref, amps_ref = refs[0], refs[1]
        pos = 2
        field_refs = refs[pos : pos + len(fields)]
        pos += len(fields)
        model_refs = refs[pos : pos + len(inputs_m)]
        pos += len(inputs_m)
        left_refs = refs[pos : pos + n_side]
        pos += n_side
        right_refs = refs[pos : pos + n_side]
        pos += n_side
        other_hbm = refs[pos : pos + len(others)]
        pos += len(others)
        n_out = blocks if kind == "blocks" else 1
        n_model = 2 if first_pass else 0
        outs = refs[pos : pos + n_out]
        pos += n_out
        model_outs = refs[pos : pos + n_model]
        pos += n_model
        buf_a, buf_b, v_buf, h_buf, stage_l, stage_r, stage_t, top, beside, sums, sem = refs[
            pos : pos + 11
        ]
        model_bufs = (h_buf, v_buf)

        steps = [ints_ref[k] for k in range(n_snaps)]
        first_row, skip, place = [ints_ref[n_snaps + k] for k in range(3)]
        inside, source_x, source_y = [
            ints_ref[n_snaps + 3 + 2 * k + shot] for k in range(3)
        ]
        window = pl.ds(pl.multiple_of(first_row, 8), rows)
        inner = pl.ds(PAD, rows)

        tile_copies = []
        if first_pass:
            tile_copies = [
                pltpu.make_async_copy(
                    ref.at[:, window], buf.at[pl.ds(reach, width)], sem.at[n]
                )
                for n, (ref, buf) in enumerate(zip(model_refs, (v_buf, h_buf)))
            ]
        else:
            tile_copies = [
                pltpu.make_async_copy(
                    ref.at[pl.ds(1, layers - 2)], buf.at[pl.ds(1, layers - 2)], sem.at[18 + n]
                )
                for n, (ref, buf) in enumerate(zip(model_refs, model_bufs))
            ]
        side_copies = []
        where = 0
        offsets = []
        for depth, (pack, layer) in zip(depths, halo_at):
            n = len(side_copies)
            side_copies.append(
                pltpu.make_async_copy(
                    left_refs[pack].at[pl.ds(layer, depth)],
                    stage_l.at[pl.ds(where, depth)],
                    sem.at[2 + n],
                )
            )
            side_copies.append(
                pltpu.make_async_copy(
                    right_refs[pack].at[pl.ds(layer, depth)],
                    stage_r.at[pl.ds(where, depth)],
                    sem.at[3 + n],
                )
            )
            offsets.append(where)
            where += depth
        if packed:
            field_copies = [pltpu.make_async_copy(field_refs[0], stage_t, sem.at[12])]
        else:
            field_copies = [
                pltpu.make_async_copy(
                    field_refs[0].at[:, window], buf_a.at[pl.ds(reach, width), inner], sem.at[12]
                ),
                pltpu.make_async_copy(
                    field_refs[1].at[:, window], buf_b.at[pl.ds(reach, width), inner], sem.at[13]
                ),
            ]
            if backward:
                n_data = data.shape[0]
                flat = refs[-2]
                field_copies.append(
                    pltpu.make_async_copy(field_refs[2], flat.at[pl.ds(0, n_data)], sem.at[14])
                )
                flat[n_data:, :] = jnp.zeros((LANES - n_data, all_rows), jnp.float32)
        other_refs = refs[pos + 11 : pos + 11 + len(others)]
        other_copies = [
            pltpu.make_async_copy(source, target, sem.at[15 + n])
            for n, (source, target) in enumerate(zip(other_hbm, other_refs))
        ]
        in_order = tile_copies + side_copies + field_copies
        if not first_pass:
            in_order = side_copies + field_copies + tile_copies
        for copy in in_order + other_copies:
            copy.start()
        beside[...] = neighbour_matrix()
        zeros = jnp.zeros((layers, PAD, LANES), jnp.float32)
        for buf in (buf_a, buf_b):
            buf[:, 0:PAD, :] = zeros
            buf[:, PAD + rows : PAD + rows + PAD, :] = zeros
        for copy in side_copies:
            copy.wait()

        def widen(stage, at, dst, first, count, row0, scale):
            def body(x, carry):
                for r0, size in spans(rows, 64):
                    code = stage[at + x, pl.ds(r0, size), :].astype(jnp.int32)
                    dst[first + x, pl.ds(row0 + r0, size), :] = code.astype(jnp.float32) * scale
                return carry

            lax.fori_loop(0, count, body, 0)

        side_scales = []
        for stage, starts in ((stage_l, (0, 1, 1, 1)), (stage_r, (reach + width,) * 4)):
            scale = decode_scale(stage, offsets[0], first_row, half_rows)
            side_scales.append(scale)
            targets = (buf_a, buf_b) + ((v_buf, h_buf) if first_pass else ())
            for dst, at, start, depth, row0, unit in zip(
                targets, offsets, starts, depths, (PAD, PAD, 0, 0),
                (scale, scale, 1.0 / FIXED, 1.0 / FIXED),
            ):
                widen(stage, at, dst, start, depth, row0, unit)
        if first_pass:
            for copy in tile_copies:
                copy.wait()

        def coefficients(x, carry):
            for r0, size in spans(rows, 64):
                at = pl.ds(r0, size)
                h_buf[x, at, :] = v_buf[x, at, :] * (1.0 + 2.0 * h_buf[x, at, :])
            return carry

        model_copies = []
        if first_pass:
            lax.fori_loop(1, layers - 1, coefficients, 0)
            model_copies = [
                pltpu.make_async_copy(
                    buf.at[pl.ds(1, layers - 2)], out.at[pl.ds(1, layers - 2)], sem.at[18 + n]
                )
                for n, (buf, out) in enumerate(zip(model_bufs, model_outs))
            ]
            for copy in model_copies:
                copy.start()
        for copy in field_copies:
            copy.wait()
        if packed:
            scale = decode_scale(stage_t, field_at[0], first_row, half_rows)
            widen(stage_t, field_at[0], buf_a, reach, width, PAD, scale)
            widen(stage_t, field_at[1], buf_b, reach, width, PAD, scale)
        surface = None
        if backward:
            widen(stage_l, offsets[-1], top, 0, 1, 0, side_scales[0])
            if packed:
                widen(stage_t, field_at[2], top, 1, 1, 0, scale)
            else:
                turned = refs[-1]
                turned[...] = flat[...].T
                top[1] = turned[window, :]
            widen(stage_r, offsets[-1], top, 2, 1, 0, side_scales[1])

        if kind in ("image", "blocks"):
            image = outs[0] if kind == "image" else refs[-1]
            image[...] = jnp.zeros_like(image)

        def record(buf, time):
            slot, found = slot_of(steps, time)
            if kind in ("image", "blocks"):
                found = found & (inside > 0)

            @pl.when(found)
            def _():
                def body(x, carry):
                    for r0, size in spans(half_rows, 64):
                        base = pl.multiple_of(PAD + skip + r0, 8)
                        at = pl.ds(r0, size)
                        value = buf[reach + x, pl.ds(base, size), :]
                        if kind in ("snaps", "waves"):
                            outs[0][slot, x, at, :] = value.astype(outs[0].dtype)
                        elif kind == "image":
                            u = other_refs[0][slot, x, at, :].astype(jnp.float32)
                            image[x, at, :] = image[x, at, :] + u * value
                        else:
                            u = value.astype(jnp.bfloat16).astype(jnp.float32)
                            image[x, at, :] = image[x, at, :] + u * other_refs[1][slot, x, at, :]
                    return carry

                lax.fori_loop(0, width, body, 0)

        src, dst = buf_a, buf_b
        coefs = (h_buf, v_buf)
        if not first_pass:
            for copy in tile_copies:
                copy.wait()
        for step in range(1, reach + 1):
            lo, hi = step, layers - step
            if backward:

                def shift(x, step=step):
                    past = x - reach + width
                    plane = past // width
                    lane = (reach - step) * width + past - plane * width
                    return plane, lax.rem(LANES - lane, LANES)

                surface = (top, shift)
            stencil_step(src, dst, coefs, lo, hi, rows, beside, sums, surface)
            if not backward:
                row8 = lax.broadcasted_iota(jnp.int32, (8, LANES), 0)
                lane8 = lax.broadcasted_iota(jnp.int32, (8, LANES), 1)

                @pl.when((source_x >= lo) & (source_x < hi) & (source_y >= 0) & (source_y < rows))
                def _(dst=dst, step=step):
                    base = pl.multiple_of((source_y // 8) * 8, 8)
                    at = pl.ds(pl.multiple_of(base + PAD, 8), 8)
                    mask = (row8 == source_y - base) & (lane8 == 0)
                    add = v_buf[source_x, pl.ds(base, 8), :] * amps_ref[shot * reach + step - 1]
                    dst[source_x, at, :] = dst[source_x, at, :] + jnp.where(mask, add, 0.0)

            if step == 1:
                for copy in other_copies[-1:]:
                    copy.wait()
                record(src, reach + 1 if backward else 1)
            src, dst = dst, src
            record(src, reach + 1 - step if backward else step + 1)

        for copy in model_copies + other_copies[:-1]:
            copy.wait()
        if kind == "blocks":
            block = half_rows // blocks
            for d, out in enumerate(outs):
                base = pl.multiple_of(lax.rem(place + d, blocks) * block, 8)

                def cut(x, carry, out=out, base=base):
                    at = pl.ds(base, block)
                    out[x] = (other_refs[0][x, at, :] + image[x, at, :]).astype(out.dtype)
                    return carry

                lax.fori_loop(0, width, cut, 0)

    any_spec = pl.BlockSpec(memory_space=pltpu.HBM)
    smem = pl.BlockSpec(memory_space=pltpu.SMEM)
    vmem = pl.BlockSpec(memory_space=pltpu.VMEM)
    shape = (width, half_rows, depth_cells)
    if kind == "blocks":
        block_shape = (width, half_rows // blocks, depth_cells)
        out_shape = (jax.ShapeDtypeStruct(block_shape, jnp.float32),)
        out_shape += (jax.ShapeDtypeStruct(block_shape, jnp.bfloat16),) * (blocks - 1)
    elif kind == "image":
        out_shape = (jax.ShapeDtypeStruct(shape, jnp.float32),)
    else:
        dtype = jnp.bfloat16 if kind == "snaps" else jnp.float32
        out_shape = (jax.ShapeDtypeStruct((n_snaps,) + shape, dtype),)
    n_model = 2 if first_pass else 0
    if first_pass:
        out_shape += (jax.ShapeDtypeStruct((layers, rows, depth_cells), jnp.float32),) * 2
    cells = layers * rows * depth_cells
    grid_buf = pltpu.VMEM((layers, rows, depth_cells), jnp.float32)
    field_buf = pltpu.VMEM((layers, rows + 2 * PAD, depth_cells), jnp.float32)
    stage_layers = field.shape[0] if packed else 1
    side = pltpu.VMEM((sum(depths), rows, depth_cells), WIRE)
    return pl.pallas_call(
        kernel,
        out_shape=out_shape,
        in_specs=[smem, smem]
        + [any_spec] * len(fields)
        + [any_spec] * (len(inputs_m) + 2 * n_side + len(others)),
        out_specs=(vmem,) * (len(out_shape) - n_model) + (any_spec,) * n_model,
        scratch_shapes=[
            field_buf, field_buf, grid_buf, grid_buf, side, side,
            pltpu.VMEM((stage_layers, rows, depth_cells), WIRE),
            pltpu.VMEM((3, rows, depth_cells), jnp.float32),
            pltpu.VMEM((2 * LANES, LANES), jnp.bfloat16),
            pltpu.VMEM((2, rows, depth_cells), jnp.float32),
            pltpu.SemaphoreType.DMA((21,)),
        ]
        + [pltpu.VMEM(other.shape, other.dtype) for other in others]
        + ([pltpu.VMEM(shape, jnp.float32)] if kind == "blocks" else [])
        + (
            [pltpu.VMEM((LANES, all_rows), jnp.float32), pltpu.VMEM((all_rows, LANES), jnp.float32)]
            if kind == "waves"
            else []
        ),
        cost_estimate=pl.CostEstimate(
            flops=15 * cells * reach, bytes_accessed=20 * cells, transcendentals=0
        ),
        compiler_params=pltpu.CompilerParams(vmem_limit_bytes=VMEM_OF_PASS),
    )(ints, amps, *fields, *inputs_m, *left, *right, *others)


def any_specs(n):
    return [pl.BlockSpec(memory_space=pltpu.HBM)] * n


def pack_rows(first, fields, ranges, groups, data):
    width, all_rows, depth_cells = fields[0].shape
    half_rows = all_rows // 2
    rows = half_rows + EDGE
    tail = 0 if data is None else 1
    sizes = [sum(hi - lo for _, lo, hi in r) + tail for r in ranges]
    n = len(fields)
    loose = [i for i in range(n) if not any(i in group for group in groups)]

    def kernel(first_ref, *refs):
        field_refs = refs[:n]
        outs = refs[n + tail : n + tail + len(ranges)]
        rest = refs[n + tail + len(ranges) :]
        wide, narrow, sem, out_sem = rest[:4]
        window = pl.ds(pl.multiple_of(first_ref[0], 8), rows)
        base, spare = spare_row(first_ref[0], half_rows)
        copies = [
            pltpu.make_async_copy(ref.at[:, window], wide.at[i], sem.at[i])
            for i, ref in enumerate(field_refs)
        ]
        for copy in copies:
            copy.start()
        started = []

        def go(source, target):
            copy = pltpu.make_async_copy(source, target, out_sem.at[len(started)])
            copy.start()
            started.append(copy)

        def code(values, scale):
            return jnp.floor(values * scale + 0.5).astype(jnp.int32).astype(WIRE)

        def put(i, scale):
            def body(x, carry):
                for r0, size in spans(rows, 64):
                    at = pl.ds(r0, size)
                    narrow[i, x, at, :] = code(wide[i, x, at, :], scale)
                return carry

            lax.fori_loop(0, width, body, 0)
            for out, pieces in zip(outs, ranges):
                where = 0
                for field, lo, hi in pieces:
                    if field == i:
                        go(narrow.at[i, pl.ds(lo, hi - lo)], out.at[pl.ds(where, hi - lo)])
                    where += hi - lo

        for number, group in enumerate(groups):
            with_data = tail and number == len(groups) - 1
            if with_data:
                flat, turned = rest[4:6]
                load = pltpu.make_async_copy(refs[n], flat.at[pl.ds(0, data.shape[0])], sem.at[n])
                load.start()
                load.wait()
                flat[data.shape[0] :, :] = jnp.zeros((LANES - data.shape[0], all_rows), jnp.float32)
                turned[...] = flat[...].T
            top = jnp.zeros((8, LANES), jnp.float32)
            for i in group:
                copies[i].wait()

                def largest(x, top, i=i):
                    for r0, size in spans(rows, 64):
                        block = jnp.abs(wide[i, x, pl.ds(r0, size), :])
                        top = jnp.maximum(top, jnp.max(block.reshape(-1, 8, LANES), axis=0))
                    return top

                top = lax.fori_loop(0, width, largest, top)
            if with_data:
                block = jnp.abs(turned[window, :])
                top = jnp.maximum(top, jnp.max(block.reshape(-1, 8, LANES), axis=0))
            top = jnp.max(top, axis=(0, 1), keepdims=True)
            scale, unit, exponent = encode_scale(top)
            header = jnp.broadcast_to(exponent * unit, (8, LANES))
            is_spare = lax.broadcasted_iota(jnp.int32, (8, LANES), 0) == spare
            for x in range(width):
                old = wide[group[0], x, pl.ds(base, 8), :]
                wide[group[0], x, pl.ds(base, 8), :] = jnp.where(is_spare, header, old)
            for i in group:
                put(i, scale)
            if with_data:
                narrow[n, 0] = code(turned[window, :], scale)
                for out, size in zip(outs, sizes):
                    go(narrow.at[n, pl.ds(0, 1)], out.at[pl.ds(size - 1, 1)])
        for i in loose:
            copies[i].wait()
            put(i, FIXED)
        for copy in started:
            copy.wait()

    n_out = sum(len(r) for r in ranges) + tail * len(ranges)
    scratch = [
        pltpu.VMEM((n, width, rows, depth_cells), jnp.float32),
        pltpu.VMEM((n + tail, width, rows, depth_cells), WIRE),
        pltpu.SemaphoreType.DMA((n + 1,)),
        pltpu.SemaphoreType.DMA((n_out,)),
    ]
    if tail:
        scratch += [
            pltpu.VMEM((LANES, all_rows), jnp.float32),
            pltpu.VMEM((all_rows, LANES), jnp.float32),
        ]
    cells = n * width * rows * depth_cells
    return pl.pallas_call(
        kernel,
        out_shape=tuple(jax.ShapeDtypeStruct((m, rows, depth_cells), WIRE) for m in sizes),
        in_specs=[pl.BlockSpec(memory_space=pltpu.SMEM)] + any_specs(n + tail),
        out_specs=tuple(any_specs(len(sizes))),
        scratch_shapes=scratch,
        cost_estimate=pl.CostEstimate(flops=cells, bytes_accessed=8 * cells, transcendentals=0),
        name="pack_rows",
    )(first, *fields, *([] if data is None else [data]))


def repack(packed, ranges):
    sizes = [sum(hi - lo for lo, hi in r) for r in ranges]
    n_out = sum(len(r) for r in ranges)

    def kernel(packed_ref, *refs):
        outs = refs[: len(ranges)]
        stage, sem, out_sem = refs[len(ranges) :]
        load = pltpu.make_async_copy(packed_ref, stage, sem.at[0])
        load.start()
        load.wait()
        started = []
        for out, pieces in zip(outs, ranges):
            where = 0
            for lo, hi in pieces:
                copy = pltpu.make_async_copy(
                    stage.at[pl.ds(lo, hi - lo)],
                    out.at[pl.ds(where, hi - lo)],
                    out_sem.at[len(started)],
                )
                copy.start()
                started.append(copy)
                where += hi - lo
        for copy in started:
            copy.wait()

    return pl.pallas_call(
        kernel,
        out_shape=tuple(jax.ShapeDtypeStruct((m,) + packed.shape[1:], packed.dtype) for m in sizes),
        in_specs=any_specs(1),
        out_specs=tuple(any_specs(len(sizes))),
        scratch_shapes=[
            pltpu.VMEM(packed.shape, packed.dtype),
            pltpu.SemaphoreType.DMA((1,)),
            pltpu.SemaphoreType.DMA((n_out,)),
        ],
        cost_estimate=pl.CostEstimate(
            flops=0, bytes_accessed=6 * packed.size, transcendentals=0
        ),
        name="repack",
    )(packed)


def on_device(
    fwd_prev,
    fwd_cur,
    bwd_next,
    bwd_cur,
    receiver_data,
    velocity_term,
    anisotropy,
    wavelet,
    shot_x,
    shot_y,
    aperture,
    snap_steps,
):
    shots = lax.axis_size("shot")
    tiles = lax.axis_size("xy")
    me = lax.axis_index("shot")
    tile = lax.axis_index("xy")
    half = shots // 2
    side = me // half
    partner = (me + half) % shots
    width, rows = fwd_prev.shape[1], fwd_prev.shape[2]
    reach = wavelet.shape[1]
    near = reach - 1
    n_snaps = snap_steps.shape[0]
    half_rows = rows // 2
    my_first = side * (half_rows - EDGE)
    their_first = (1 - side) * (half_rows - EDGE)
    across = [(i, (i + half) % shots) for i in range(shots)]
    up = [(i, i + 1) for i in range(tiles - 1)]
    down = [(i + 1, i) for i in range(tiles - 1)]
    u0, u1, w9, w8 = fwd_prev[0], fwd_cur[0], bwd_next[0], bwd_cur[0]

    data = receiver_data[0].reshape(reach * width, rows)

    def at(first):
        return jnp.reshape(first, (1,)).astype(jnp.int32)

    whole = ((0, 0, width), (1, 0, width))
    (send_w,) = pack_rows(at(their_first), (w8, w9), (whole,), ((0, 1),), data)
    import_w = lax.ppermute(send_w, "shot", across)

    def sides(fields, depths, groups, data):
        send_up, send_down = pack_rows(
            at(my_first), fields,
            (
                [(i, width - d, width) for i, d in enumerate(depths)],
                [(i, 0, d) for i, d in enumerate(depths)],
            ),
            groups, data,
        )
        from_left = lax.ppermute(send_up, "xy", up)
        from_right = lax.ppermute(send_down, "xy", down)
        return from_left, from_right

    left, right = sides(
        (u1, u0, velocity_term, anisotropy), (reach, near, near, near), ((0, 1),), None
    )
    left_l, right_l = sides((w8, w9), (reach, near), ((0, 1),), data)
    (send_u,) = pack_rows(at(their_first), (u1, u0), (whole,), ((0, 1),), None)
    import_u = lax.ppermute(send_u, "shot", across)

    two = jnp.stack([me, partner])
    chosen = (jnp.arange(shots, dtype=jnp.int32)[None] == two[:, None]).astype(jnp.int32)
    source_x = jnp.sum(chosen * shot_x[None], axis=1) - tile * width + reach
    source_y = jnp.sum(chosen * shot_y[None], axis=1) - my_first
    here = jnp.any(aperture == tile, axis=1).astype(jnp.int32)
    inside = jnp.sum(chosen * here[None], axis=1)
    amps = jnp.sum(jnp.where(chosen[:, :, None] > 0, wavelet[None], 0.0), axis=1).reshape(-1)
    places = jnp.stack([my_first, side * EDGE, me % half])
    ints = jnp.concatenate([snap_steps, places, inside, source_x, source_y]).astype(jnp.int32)
    common = dict(half_rows=half_rows, reach=reach, n_snaps=n_snaps)
    at_v, at_a = (0, reach + near), (0, reach + 2 * near)
    snaps, *model = wave_pass(
        "snaps", (u1, u0), None, velocity_term, anisotropy, [left], [right],
        ((0, 0), (0, reach), at_v, at_a), 0, ints, amps, **common,
    )

    def from_sides(packed, tail):
        ends = [(2 * width, 2 * width + 1)] if tail else []
        send_up, send_down = repack(
            packed,
            (
                [(width - reach, width), (2 * width - near, 2 * width)] + ends,
                [(0, reach), (width, width + near)] + ends,
            ),
        )
        from_left = lax.ppermute(send_up, "xy", up)
        from_right = lax.ppermute(send_down, "xy", down)
        return from_left, from_right

    (waves,) = wave_pass(
        "waves", (w8, w9), None, velocity_term, anisotropy, [left_l], [right_l],
        ((0, 0), (0, reach), (0, reach + near)),
        1, ints, amps, data=data, model=model, **common,
    )
    left_w, right_w = from_sides(import_w, True)
    (image,) = wave_pass(
        "image", import_w, (0, width, 2 * width), velocity_term, anisotropy,
        [left_w], [right_w], ((0, 0), (0, reach), (0, reach + near)),
        0, ints, amps, others=(snaps,), model=model, **common,
    )
    left_u, right_u = from_sides(import_u, False)
    blocks = wave_pass(
        "blocks", import_u, (0, width), velocity_term, anisotropy,
        [left_u], [right_u], ((0, 0), (0, reach)),
        1, ints, amps, blocks=half, others=(image, waves), model=model, **common,
    )
    total = blocks[0]
    for d in range(1, half):
        route = [(i, (i // half) * half + (i % half + d) % half) for i in range(shots)]
        arrived = lax.ppermute(blocks[d], "shot", route)
        total = total + arrived.astype(jnp.float32)
    return total


def solution(mesh):
    in_specs = (
        P("shot", "xy", None, None),
        P("shot", "xy", None, None),
        P("shot", "xy", None, None),
        P("shot", "xy", None, None),
        P("shot", None, "xy", None),
        P("xy", None, None),
        P("xy", None, None),
        P(),
        P(),
        P(),
        P(),
        P(),
    )
    out_specs = P("xy", "shot", None)

    return jax.shard_map(
        on_device, mesh=mesh, in_specs=in_specs, out_specs=out_specs, check_vma=False
    )
```

```python
import jax
import jax.numpy as jnp
from jax import lax
from jax.experimental import pallas as pl
from jax.experimental.pallas import tpu as pltpu
from jax.sharding import PartitionSpec as P


PAD = 8
EDGE = 8
LANES = 128
BY_MATRIX = ((True, False), (True, True))
CHUNK = 32
VMEM_OF_PASS = 67043328
WIRE = jnp.int16
STEPS_OF_SCALE = (32, 16, 8, 4, 2, 1)
FIXED = 65536.0


def spans(rows, chunk):
    return [(r0, min(chunk, rows - r0)) for r0 in range(0, rows, chunk)]


def neighbour_matrix():
    row = lax.broadcasted_iota(jnp.int32, (2 * LANES, LANES), 0)
    column = lax.broadcasted_iota(jnp.int32, (2 * LANES, LANES), 1)
    row = jnp.where(row >= LANES, row - LANES, row)
    beside = (row - column == 1) | (column - row == 1)
    return jnp.where(beside, 1.0, jnp.where(row == column, -2.0, 0.0)).astype(jnp.bfloat16)


def stencil_step(src, dst, coefs, lo, hi, rows, beside, sums, surface=None):
    hor, vel = coefs
    by_matrix = BY_MATRIX[surface is not None]

    def vertical_sums(x, j):
        for r0, size in spans(rows, 144):
            c = src[x, pl.ds(PAD + r0, size), :]
            high = c.astype(jnp.bfloat16)
            low = (c - high.astype(jnp.float32)).astype(jnp.bfloat16)
            sums[j, pl.ds(r0, size), :] = jnp.dot(
                jnp.concatenate([high, low], axis=1), beside[...],
                preferred_element_type=jnp.float32,
            )

    def ahead(x):
        for j in range(2):
            if by_matrix[j]:
                vertical_sums(x + j, j)

    def body(i, carry):
        x = lo + 2 * i
        if surface is None:
            ahead(x)
        shifts = [None, None] if surface is None else [surface[1](x), surface[1](x + 1)]
        for r0, size in spans(rows, CHUNK):
            at = pl.ds(PAD + r0, size)
            here = pl.ds(r0, size)
            lane = lax.broadcasted_iota(jnp.int32, (size, LANES), 1)
            c = [src[x - 1 + j, at, :] for j in range(4)]
            for j in range(2):
                mid = c[j + 1]
                lateral = c[j] + c[j + 2]
                lateral = lateral + src[x + j, pl.ds(PAD + r0 - 1, size), :]
                lateral = lateral + src[x + j, pl.ds(PAD + r0 + 1, size), :]
                data = 0.0
                if surface is not None:
                    plane, shift = shifts[j]
                    data = pltpu.roll(surface[0][plane, here, :], shift, 1)
                if by_matrix[j]:
                    vertical = sums[j, here, :]
                    if surface is not None:
                        vertical = vertical + jnp.where(lane == 0, data, 0.0)
                else:
                    above = jnp.where(lane == 0, data, pltpu.roll(mid, 1, 1))
                    deeper = jnp.where(lane == LANES - 1, 0.0, pltpu.roll(mid, LANES - 1, 1))
                    vertical = above + deeper - (mid + mid)
                twice = mid + mid
                new = twice - dst[x + j, at, :]
                new = new + hor[x + j, here, :] * (lateral - (twice + twice))
                new = new + vel[x + j, here, :] * vertical
                dst[x + j, at, :] = new
        if surface is not None:
            ahead(jnp.minimum(x + 2, hi - 2))
        return carry

    if surface is not None:
        ahead(lo)
    lax.fori_loop(0, (hi - lo) // 2, body, 0)


def spare_row(first, half_rows):
    return pl.multiple_of(jnp.where(first == 0, half_rows, 0), 8), jnp.where(first == 0, 7, 0)


def encode_scale(top):
    up, down, exponent = jnp.ones_like(top), jnp.ones_like(top), jnp.zeros_like(top)
    for j in STEPS_OF_SCALE:
        more = top * 2.0**j
        fits = more < 15.9
        top = jnp.where(fits, more, top)
        up = jnp.where(fits, up * 2.0**j, up)
        down = jnp.where(fits, down * 2.0**-j, down)
        exponent = jnp.where(fits, exponent + j, exponent)
    return up * 2048.0, down / 2048.0, exponent


def decode_scale(stage, layer, first, half_rows):
    base, spare = spare_row(first, half_rows)
    block = stage[layer, pl.ds(base, 8), :].astype(jnp.int32).astype(jnp.float32)
    held = lax.broadcasted_iota(jnp.int32, (8, LANES), 0) == spare
    exponent = jnp.max(jnp.where(held, block, 0.0), axis=(0, 1), keepdims=True)
    scale = jnp.full_like(exponent, 1.0 / 2048.0)
    for j in STEPS_OF_SCALE:
        holds = exponent >= j
        scale = jnp.where(holds, scale * 2.0**-j, scale)
        exponent = jnp.where(holds, exponent - j, exponent)
    return scale


def slot_of(steps, time):
    slot = jnp.int32(0)
    found = jnp.int32(0)
    for k, step in enumerate(steps):
        hit = (step == time).astype(jnp.int32)
        slot = slot + hit * k
        found = found + hit
    return slot, found > 0


def wave_pass(kind, field, field_at, vel, ani, left, right, halo_at, shot, ints, amps, half_rows, reach,
              n_snaps, blocks=1, others=(), data=None, model=None):
    width, all_rows, depth_cells = vel.shape
    rows = half_rows + EDGE
    layers = width + 2 * reach
    near = reach - 1
    backward = kind in ("waves", "image")
    packed = not isinstance(field, tuple)
    fields = [field] if packed else list(field) + ([data] if backward else [])
    first_pass = model is None
    stacks = kind in ("snaps", "waves")
    depths = (reach, near) + ((near, near) if first_pass else ()) + ((1,) if backward else ())
    inputs_m = [vel, ani] if first_pass else list(model)
    n_side = len(left)

    def kernel(*refs):
        ints_ref, amps_ref = refs[0], refs[1]
        pos = 2
        field_refs = refs[pos : pos + len(fields)]
        pos += len(fields)
        model_refs = refs[pos : pos + len(inputs_m)]
        pos += len(inputs_m)
        left_refs = refs[pos : pos + n_side]
        pos += n_side
        right_refs = refs[pos : pos + n_side]
        pos += n_side
        other_hbm = refs[pos : pos + len(others)]
        pos += len(others)
        n_out = blocks if kind == "blocks" else 1
        n_model = 2 if first_pass else 0
        outs = refs[pos : pos + n_out]
        pos += n_out
        model_outs = refs[pos : pos + n_model]
        pos += n_model
        buf_a, buf_b, v_buf, h_buf, stage_l, stage_r, stage_t, top, beside, sums, sem = refs[
            pos : pos + 11
        ]
        model_bufs = (h_buf, v_buf)

        steps = [ints_ref[k] for k in range(n_snaps)]
        first_row, skip, place = [ints_ref[n_snaps + k] for k in range(3)]
        inside, source_x, source_y = [
            ints_ref[n_snaps + 3 + 2 * k + shot] for k in range(3)
        ]
        window = pl.ds(pl.multiple_of(first_row, 8), rows)
        inner = pl.ds(PAD, rows)

        tile_copies = []
        if first_pass:
            tile_copies = [
                pltpu.make_async_copy(
                    ref.at[:, window], buf.at[pl.ds(reach, width)], sem.at[n]
                )
                for n, (ref, buf) in enumerate(zip(model_refs, (v_buf, h_buf)))
            ]
        else:
            tile_copies = [
                pltpu.make_async_copy(
                    ref.at[pl.ds(1, layers - 2)], buf.at[pl.ds(1, layers - 2)], sem.at[18 + n]
                )
                for n, (ref, buf) in enumerate(zip(model_refs, model_bufs))
            ]
        side_copies = []
        where = 0
        offsets = []
        for depth, (pack, layer) in zip(depths, halo_at):
            n = len(side_copies)
            side_copies.append(
                pltpu.make_async_copy(
                    left_refs[pack].at[pl.ds(layer, depth)],
                    stage_l.at[pl.ds(where, depth)],
                    sem.at[2 + n],
                )
            )
            side_copies.append(
                pltpu.make_async_copy(
                    right_refs[pack].at[pl.ds(layer, depth)],
                    stage_r.at[pl.ds(where, depth)],
                    sem.at[3 + n],
                )
            )
            offsets.append(where)
            where += depth
        if packed:
            field_copies = [pltpu.make_async_copy(field_refs[0], stage_t, sem.at[12])]
        else:
            field_copies = [
                pltpu.make_async_copy(
                    field_refs[0].at[:, window], buf_a.at[pl.ds(reach, width), inner], sem.at[12]
                ),
                pltpu.make_async_copy(
                    field_refs[1].at[:, window], buf_b.at[pl.ds(reach, width), inner], sem.at[13]
                ),
            ]
            if backward:
                n_data = data.shape[0]
                flat = refs[-2]
                field_copies.append(
                    pltpu.make_async_copy(field_refs[2], flat.at[pl.ds(0, n_data)], sem.at[14])
                )
                flat[n_data:, :] = jnp.zeros((LANES - n_data, all_rows), jnp.float32)
        held = refs[pos + 11] if stacks else None
        out_copies = []
        other_refs = refs[pos + 11 : pos + 11 + len(others)]
        other_copies = [
            pltpu.make_async_copy(source, target, sem.at[15 + n])
            for n, (source, target) in enumerate(zip(other_hbm, other_refs))
        ]
        in_order = tile_copies + side_copies + field_copies
        if not first_pass:
            in_order = side_copies + field_copies + tile_copies
        for copy in in_order + other_copies:
            copy.start()
        beside[...] = neighbour_matrix()
        zeros = jnp.zeros((layers, PAD, LANES), jnp.float32)
        for buf in (buf_a, buf_b):
            buf[:, 0:PAD, :] = zeros
            buf[:, PAD + rows : PAD + rows + PAD, :] = zeros
        for copy in side_copies:
            copy.wait()

        def widen(stage, at, dst, first, count, row0, scale):
            def body(x, carry):
                for r0, size in spans(rows, 64):
                    code = stage[at + x, pl.ds(r0, size), :].astype(jnp.int32)
                    dst[first + x, pl.ds(row0 + r0, size), :] = code.astype(jnp.float32) * scale
                return carry

            lax.fori_loop(0, count, body, 0)

        side_scales = []
        for stage, starts in ((stage_l, (0, 1, 1, 1)), (stage_r, (reach + width,) * 4)):
            scale = decode_scale(stage, offsets[0], first_row, half_rows)
            side_scales.append(scale)
            targets = (buf_a, buf_b) + ((v_buf, h_buf) if first_pass else ())
            for dst, at, start, depth, row0, unit in zip(
                targets, offsets, starts, depths, (PAD, PAD, 0, 0),
                (scale, scale, 1.0 / FIXED, 1.0 / FIXED),
            ):
                widen(stage, at, dst, start, depth, row0, unit)
        if first_pass:
            for copy in tile_copies:
                copy.wait()

        def coefficients(x, carry):
            for r0, size in spans(rows, 64):
                at = pl.ds(r0, size)
                h_buf[x, at, :] = v_buf[x, at, :] * (1.0 + 2.0 * h_buf[x, at, :])
            return carry

        model_copies = []
        if first_pass:
            lax.fori_loop(1, layers - 1, coefficients, 0)
            model_copies = [
                pltpu.make_async_copy(
                    buf.at[pl.ds(1, layers - 2)], out.at[pl.ds(1, layers - 2)], sem.at[18 + n]
                )
                for n, (buf, out) in enumerate(zip(model_bufs, model_outs))
            ]
            for copy in model_copies:
                copy.start()
        for copy in field_copies:
            copy.wait()
        if packed:
            scale = decode_scale(stage_t, field_at[0], first_row, half_rows)
            widen(stage_t, field_at[0], buf_a, reach, width, PAD, scale)
            widen(stage_t, field_at[1], buf_b, reach, width, PAD, scale)
        surface = None
        if backward:
            widen(stage_l, offsets[-1], top, 0, 1, 0, side_scales[0])
            if packed:
                widen(stage_t, field_at[2], top, 1, 1, 0, scale)
            else:
                turned = refs[-1]
                turned[...] = flat[...].T
                top[1] = turned[window, :]
            widen(stage_r, offsets[-1], top, 2, 1, 0, side_scales[1])

        if kind in ("image", "blocks"):
            image = outs[0] if kind == "image" else refs[-1]
            image[...] = jnp.zeros_like(image)

        def record(buf, time):
            slot, found = slot_of(steps, time)
            if kind in ("image", "blocks"):
                found = found & (inside > 0)

            @pl.when(found)
            def _():
                def body(x, carry):
                    for r0, size in spans(half_rows, 64):
                        base = pl.multiple_of(PAD + skip + r0, 8)
                        at = pl.ds(r0, size)
                        value = buf[reach + x, pl.ds(base, size), :]
                        if stacks:
                            held[slot, x, at, :] = value.astype(held.dtype)
                        elif kind == "image":
                            u = other_refs[0][slot, x, at, :].astype(jnp.float32)
                            image[x, at, :] = image[x, at, :] + u * value
                        else:
                            u = value.astype(jnp.bfloat16).astype(jnp.float32)
                            image[x, at, :] = image[x, at, :] + u * other_refs[1][slot, x, at, :]
                    return carry

                lax.fori_loop(0, width, body, 0)

            done = time - 1 if backward else time - 1 - (reach + 1 - n_snaps)
            if stacks and 0 <= done < n_snaps:
                copy = pltpu.make_async_copy(held.at[done], outs[0].at[done], sem.at[21 + done])
                copy.start()
                out_copies.append(copy)

        src, dst = buf_a, buf_b
        coefs = (h_buf, v_buf)
        if not first_pass:
            for copy in tile_copies:
                copy.wait()
        for step in range(1, reach + 1):
            lo, hi = step, layers - step
            if backward:

                def shift(x, step=step):
                    past = x - reach + width
                    plane = past // width
                    lane = (reach - step) * width + past - plane * width
                    return plane, lax.rem(LANES - lane, LANES)

                surface = (top, shift)
            stencil_step(src, dst, coefs, lo, hi, rows, beside, sums, surface)
            if not backward:
                row8 = lax.broadcasted_iota(jnp.int32, (8, LANES), 0)
                lane8 = lax.broadcasted_iota(jnp.int32, (8, LANES), 1)

                @pl.when((source_x >= lo) & (source_x < hi) & (source_y >= 0) & (source_y < rows))
                def _(dst=dst, step=step):
                    base = pl.multiple_of((source_y // 8) * 8, 8)
                    at = pl.ds(pl.multiple_of(base + PAD, 8), 8)
                    mask = (row8 == source_y - base) & (lane8 == 0)
                    add = v_buf[source_x, pl.ds(base, 8), :] * amps_ref[shot * reach + step - 1]
                    dst[source_x, at, :] = dst[source_x, at, :] + jnp.where(mask, add, 0.0)

            if step == 1:
                for copy in other_copies[-1:]:
                    copy.wait()
                record(src, reach + 1 if backward else 1)
            src, dst = dst, src
            record(src, reach + 1 - step if backward else step + 1)

        for copy in model_copies + other_copies[:-1] + out_copies:
            copy.wait()
        if kind == "blocks":
            block = half_rows // blocks
            for d, out in enumerate(outs):
                base = pl.multiple_of(lax.rem(place + d, blocks) * block, 8)

                def cut(x, carry, out=out, base=base):
                    at = pl.ds(base, block)
                    out[x] = (other_refs[0][x, at, :] + image[x, at, :]).astype(out.dtype)
                    return carry

                lax.fori_loop(0, width, cut, 0)

    any_spec = pl.BlockSpec(memory_space=pltpu.HBM)
    smem = pl.BlockSpec(memory_space=pltpu.SMEM)
    vmem = pl.BlockSpec(memory_space=pltpu.VMEM)
    shape = (width, half_rows, depth_cells)
    if kind == "blocks":
        block_shape = (width, half_rows // blocks, depth_cells)
        out_shape = (jax.ShapeDtypeStruct(block_shape, jnp.float32),)
        out_shape += (jax.ShapeDtypeStruct(block_shape, jnp.bfloat16),) * (blocks - 1)
    elif kind == "image":
        out_shape = (jax.ShapeDtypeStruct(shape, jnp.float32),)
    else:
        dtype = jnp.bfloat16 if kind == "snaps" else jnp.float32
        out_shape = (jax.ShapeDtypeStruct((n_snaps,) + shape, dtype),)
    n_model = 2 if first_pass else 0
    if first_pass:
        out_shape += (jax.ShapeDtypeStruct((layers, rows, depth_cells), jnp.float32),) * 2
    cells = layers * rows * depth_cells
    grid_buf = pltpu.VMEM((layers, rows, depth_cells), jnp.float32)
    field_buf = pltpu.VMEM((layers, rows + 2 * PAD, depth_cells), jnp.float32)
    stage_layers = field.shape[0] if packed else 1
    side = pltpu.VMEM((sum(depths), rows, depth_cells), WIRE)
    return pl.pallas_call(
        kernel,
        out_shape=out_shape,
        in_specs=[smem, smem]
        + [any_spec] * len(fields)
        + [any_spec] * (len(inputs_m) + 2 * n_side + len(others)),
        out_specs=(any_spec if stacks else vmem,) * (len(out_shape) - n_model) + (any_spec,) * n_model,
        scratch_shapes=[
            field_buf, field_buf, grid_buf, grid_buf, side, side,
            pltpu.VMEM((stage_layers, rows, depth_cells), WIRE),
            pltpu.VMEM((3, rows, depth_cells), jnp.float32),
            pltpu.VMEM((2 * LANES, LANES), jnp.bfloat16),
            pltpu.VMEM((2, rows, depth_cells), jnp.float32),
            pltpu.SemaphoreType.DMA((21 + n_snaps,)),
        ]
        + ([pltpu.VMEM(out_shape[0].shape, out_shape[0].dtype)] if stacks else [])
        + [pltpu.VMEM(other.shape, other.dtype) for other in others]
        + ([pltpu.VMEM(shape, jnp.float32)] if kind == "blocks" else [])
        + (
            [pltpu.VMEM((LANES, all_rows), jnp.float32), pltpu.VMEM((all_rows, LANES), jnp.float32)]
            if kind == "waves"
            else []
        ),
        cost_estimate=pl.CostEstimate(
            flops=15 * cells * reach, bytes_accessed=20 * cells, transcendentals=0
        ),
        compiler_params=pltpu.CompilerParams(vmem_limit_bytes=VMEM_OF_PASS),
    )(ints, amps, *fields, *inputs_m, *left, *right, *others)


def any_specs(n):
    return [pl.BlockSpec(memory_space=pltpu.HBM)] * n


def pack_rows(first, fields, ranges, groups, data):
    width, all_rows, depth_cells = fields[0].shape
    half_rows = all_rows // 2
    rows = half_rows + EDGE
    tail = 0 if data is None else 1
    sizes = [sum(hi - lo for _, lo, hi in r) + tail for r in ranges]
    n = len(fields)
    loose = [i for i in range(n) if not any(i in group for group in groups)]

    def kernel(first_ref, *refs):
        field_refs = refs[:n]
        outs = refs[n + tail : n + tail + len(ranges)]
        rest = refs[n + tail + len(ranges) :]
        wide, narrow, sem, out_sem = rest[:4]
        window = pl.ds(pl.multiple_of(first_ref[0], 8), rows)
        base, spare = spare_row(first_ref[0], half_rows)
        copies = [
            pltpu.make_async_copy(ref.at[:, window], wide.at[i], sem.at[i])
            for i, ref in enumerate(field_refs)
        ]
        for copy in copies:
            copy.start()
        started = []

        def go(source, target):
            copy = pltpu.make_async_copy(source, target, out_sem.at[len(started)])
            copy.start()
            started.append(copy)

        def code(values, scale):
            return jnp.floor(values * scale + 0.5).astype(jnp.int32).astype(WIRE)

        def put(i, scale):
            def body(x, carry):
                for r0, size in spans(rows, 64):
                    at = pl.ds(r0, size)
                    narrow[i, x, at, :] = code(wide[i, x, at, :], scale)
                return carry

            lax.fori_loop(0, width, body, 0)
            for out, pieces in zip(outs, ranges):
                where = 0
                for field, lo, hi in pieces:
                    if field == i:
                        go(narrow.at[i, pl.ds(lo, hi - lo)], out.at[pl.ds(where, hi - lo)])
                    where += hi - lo

        for number, group in enumerate(groups):
            with_data = tail and number == len(groups) - 1
            if with_data:
                flat, turned = rest[4:6]
                load = pltpu.make_async_copy(refs[n], flat.at[pl.ds(0, data.shape[0])], sem.at[n])
                load.start()
                load.wait()
                flat[data.shape[0] :, :] = jnp.zeros((LANES - data.shape[0], all_rows), jnp.float32)
                turned[...] = flat[...].T
            top = jnp.zeros((8, LANES), jnp.float32)
            for i in group:
                copies[i].wait()

                def largest(x, top, i=i):
                    for r0, size in spans(rows, 64):
                        block = jnp.abs(wide[i, x, pl.ds(r0, size), :])
                        top = jnp.maximum(top, jnp.max(block.reshape(-1, 8, LANES), axis=0))
                    return top

                top = lax.fori_loop(0, width, largest, top)
            if with_data:
                block = jnp.abs(turned[window, :])
                top = jnp.maximum(top, jnp.max(block.reshape(-1, 8, LANES), axis=0))
            top = jnp.max(top, axis=(0, 1), keepdims=True)
            scale, unit, exponent = encode_scale(top)
            header = jnp.broadcast_to(exponent * unit, (8, LANES))
            is_spare = lax.broadcasted_iota(jnp.int32, (8, LANES), 0) == spare
            for x in range(width):
                old = wide[group[0], x, pl.ds(base, 8), :]
                wide[group[0], x, pl.ds(base, 8), :] = jnp.where(is_spare, header, old)
            for i in group:
                put(i, scale)
            if with_data:
                narrow[n, 0] = code(turned[window, :], scale)
                for out, size in zip(outs, sizes):
                    go(narrow.at[n, pl.ds(0, 1)], out.at[pl.ds(size - 1, 1)])
        for i in loose:
            copies[i].wait()
            put(i, FIXED)
        for copy in started:
            copy.wait()

    n_out = sum(len(r) for r in ranges) + tail * len(ranges)
    scratch = [
        pltpu.VMEM((n, width, rows, depth_cells), jnp.float32),
        pltpu.VMEM((n + tail, width, rows, depth_cells), WIRE),
        pltpu.SemaphoreType.DMA((n + 1,)),
        pltpu.SemaphoreType.DMA((n_out,)),
    ]
    if tail:
        scratch += [
            pltpu.VMEM((LANES, all_rows), jnp.float32),
            pltpu.VMEM((all_rows, LANES), jnp.float32),
        ]
    cells = n * width * rows * depth_cells
    return pl.pallas_call(
        kernel,
        out_shape=tuple(jax.ShapeDtypeStruct((m, rows, depth_cells), WIRE) for m in sizes),
        in_specs=[pl.BlockSpec(memory_space=pltpu.SMEM)] + any_specs(n + tail),
        out_specs=tuple(any_specs(len(sizes))),
        scratch_shapes=scratch,
        cost_estimate=pl.CostEstimate(flops=cells, bytes_accessed=8 * cells, transcendentals=0),
        name="pack_rows",
    )(first, *fields, *([] if data is None else [data]))


def repack(packed, ranges):
    sizes = [sum(hi - lo for lo, hi in r) for r in ranges]
    n_out = sum(len(r) for r in ranges)

    def kernel(packed_ref, *refs):
        outs = refs[: len(ranges)]
        stage, sem, out_sem = refs[len(ranges) :]
        load = pltpu.make_async_copy(packed_ref, stage, sem.at[0])
        load.start()
        load.wait()
        started = []
        for out, pieces in zip(outs, ranges):
            where = 0
            for lo, hi in pieces:
                copy = pltpu.make_async_copy(
                    stage.at[pl.ds(lo, hi - lo)],
                    out.at[pl.ds(where, hi - lo)],
                    out_sem.at[len(started)],
                )
                copy.start()
                started.append(copy)
                where += hi - lo
        for copy in started:
            copy.wait()

    return pl.pallas_call(
        kernel,
        out_shape=tuple(jax.ShapeDtypeStruct((m,) + packed.shape[1:], packed.dtype) for m in sizes),
        in_specs=any_specs(1),
        out_specs=tuple(any_specs(len(sizes))),
        scratch_shapes=[
            pltpu.VMEM(packed.shape, packed.dtype),
            pltpu.SemaphoreType.DMA((1,)),
            pltpu.SemaphoreType.DMA((n_out,)),
        ],
        cost_estimate=pl.CostEstimate(
            flops=0, bytes_accessed=6 * packed.size, transcendentals=0
        ),
        name="repack",
    )(packed)


def on_device(
    fwd_prev,
    fwd_cur,
    bwd_next,
    bwd_cur,
    receiver_data,
    velocity_term,
    anisotropy,
    wavelet,
    shot_x,
    shot_y,
    aperture,
    snap_steps,
):
    shots = lax.axis_size("shot")
    tiles = lax.axis_size("xy")
    me = lax.axis_index("shot")
    tile = lax.axis_index("xy")
    half = shots // 2
    side = me // half
    partner = (me + half) % shots
    width, rows = fwd_prev.shape[1], fwd_prev.shape[2]
    reach = wavelet.shape[1]
    near = reach - 1
    n_snaps = snap_steps.shape[0]
    half_rows = rows // 2
    my_first = side * (half_rows - EDGE)
    their_first = (1 - side) * (half_rows - EDGE)
    across = [(i, (i + half) % shots) for i in range(shots)]
    up = [(i, i + 1) for i in range(tiles - 1)]
    down = [(i + 1, i) for i in range(tiles - 1)]
    u0, u1, w9, w8 = fwd_prev[0], fwd_cur[0], bwd_next[0], bwd_cur[0]

    data = receiver_data[0].reshape(reach * width, rows)

    def at(first):
        return jnp.reshape(first, (1,)).astype(jnp.int32)

    whole = ((0, 0, width), (1, 0, width))
    (send_w,) = pack_rows(at(their_first), (w8, w9), (whole,), ((0, 1),), data)
    import_w = lax.ppermute(send_w, "shot", across)

    def sides(fields, depths, groups, data):
        send_up, send_down = pack_rows(
            at(my_first), fields,
            (
                [(i, width - d, width) for i, d in enumerate(depths)],
                [(i, 0, d) for i, d in enumerate(depths)],
            ),
            groups, data,
        )
        from_left = lax.ppermute(send_up, "xy", up)
        from_right = lax.ppermute(send_down, "xy", down)
        return from_left, from_right

    left, right = sides(
        (u1, u0, velocity_term, anisotropy), (reach, near, near, near), ((0, 1),), None
    )
    left_l, right_l = sides((w8, w9), (reach, near), ((0, 1),), data)
    (send_u,) = pack_rows(at(their_first), (u1, u0), (whole,), ((0, 1),), None)
    import_u = lax.ppermute(send_u, "shot", across)

    two = jnp.stack([me, partner])
    chosen = (jnp.arange(shots, dtype=jnp.int32)[None] == two[:, None]).astype(jnp.int32)
    source_x = jnp.sum(chosen * shot_x[None], axis=1) - tile * width + reach
    source_y = jnp.sum(chosen * shot_y[None], axis=1) - my_first
    here = jnp.any(aperture == tile, axis=1).astype(jnp.int32)
    inside = jnp.sum(chosen * here[None], axis=1)
    amps = jnp.sum(jnp.where(chosen[:, :, None] > 0, wavelet[None], 0.0), axis=1).reshape(-1)
    places = jnp.stack([my_first, side * EDGE, me % half])
    ints = jnp.concatenate([snap_steps, places, inside, source_x, source_y]).astype(jnp.int32)
    common = dict(half_rows=half_rows, reach=reach, n_snaps=n_snaps)
    at_v, at_a = (0, reach + near), (0, reach + 2 * near)
    snaps, *model = wave_pass(
        "snaps", (u1, u0), None, velocity_term, anisotropy, [left], [right],
        ((0, 0), (0, reach), at_v, at_a), 0, ints, amps, **common,
    )

    def from_sides(packed, tail):
        ends = [(2 * width, 2 * width + 1)] if tail else []
        send_up, send_down = repack(
            packed,
            (
                [(width - reach, width), (2 * width - near, 2 * width)] + ends,
                [(0, reach), (width, width + near)] + ends,
            ),
        )
        from_left = lax.ppermute(send_up, "xy", up)
        from_right = lax.ppermute(send_down, "xy", down)
        return from_left, from_right

    (waves,) = wave_pass(
        "waves", (w8, w9), None, velocity_term, anisotropy, [left_l], [right_l],
        ((0, 0), (0, reach), (0, reach + near)),
        1, ints, amps, data=data, model=model, **common,
    )
    left_w, right_w = from_sides(import_w, True)
    (image,) = wave_pass(
        "image", import_w, (0, width, 2 * width), velocity_term, anisotropy,
        [left_w], [right_w], ((0, 0), (0, reach), (0, reach + near)),
        0, ints, amps, others=(snaps,), model=model, **common,
    )
    left_u, right_u = from_sides(import_u, False)
    blocks = wave_pass(
        "blocks", import_u, (0, width), velocity_term, anisotropy,
        [left_u], [right_u], ((0, 0), (0, reach)),
        1, ints, amps, blocks=half, others=(image, waves), model=model, **common,
    )
    total = blocks[0]
    for d in range(1, half):
        route = [(i, (i // half) * half + (i % half + d) % half) for i in range(shots)]
        arrived = lax.ppermute(blocks[d], "shot", route)
        total = total + arrived.astype(jnp.float32)
    return total


def solution(mesh):
    in_specs = (
        P("shot", "xy", None, None),
        P("shot", "xy", None, None),
        P("shot", "xy", None, None),
        P("shot", "xy", None, None),
        P("shot", None, "xy", None),
        P("xy", None, None),
        P("xy", None, None),
        P(),
        P(),
        P(),
        P(),
        P(),
    )
    out_specs = P("xy", "shot", None)

    return jax.shard_map(
        on_device, mesh=mesh, in_specs=in_specs, out_specs=out_specs, check_vma=False
    )
```
